32 devices in a mesh: row: 4 (over y, core), col: 8 (over z, x).
Axes of the slice: x: 2, y: 2, z: 4, core: 2. Of those that a mesh axis runs over, the one named last changes fastest.
Arguments:
- objects: float32 [2, 2, 1024, 2048], P(None, None, 'row', 'col'), may hold values from -5 to 5
- probe: float32 [2, 256, 256], replicated, may hold values from -6 to 6
- prev_partial: float32 [4, 8, 2, 256, 256], P('row', 'col'), may hold values from -6 to 6
- offsets: int32 [4, 8, 1, 2], P('row', 'col'), may hold values from 0 to 128
- counts: int32 [4, 8], P('row', 'col'), may hold values from 0 to 1
- amplitudes: float32 [4, 8, 1, 256, 256], P('row', 'col'), may hold values from 1 to 2.5
Outputs:
- new_objects: float32 [2, 2, 1024, 2048], P(None, None, 'row', 'col')
- new_probe: float32 [2, 256, 256], replicated
- new_partial: float32 [4, 8, 2, 256, 256], P('row', 'col')
The draws below stay inside these ranges and needn't reach their ends.
All inputs are finite; a program needn't handle non-finite values.
Results may differ from the reference program's by a relative error of at most 0.0003.
Values sent between devices are 32-bit elements; how exact they have to be, the bound alone decides.
A program may use at most 64 MiB of HBM per device.

```python
import math
import jax
import jax.numpy as jnp
from jax import lax

WIN = 256
HALO = 64
TILE = 256
PAT = 1
NY = 1024
NX = 2048
N_ROW = 4
N_COL = 8


def with_ends(drawn, stream_key, low, top_value):
    shape = drawn.shape
    place = [jax.random.randint(jax.random.fold_in(stream_key, axis), (), 0, shape[axis]) for axis in range(len(shape))]
    drawn = drawn.at[tuple(place)].set(low)
    longest = shape.index(max(shape))
    place[longest] = (place[longest] + 1) % shape[longest]
    return drawn.at[tuple(place)].set(top_value)


def shard_levels(stream_key, shape, shards, least, high):
    def one(dim, parts):
        draws = jax.random.uniform(jax.random.fold_in(jax.random.fold_in(stream_key, 6), dim), (parts,), jnp.float32, least / len(shards), high / len(shards))
        return jnp.repeat(jnp.exp(draws), shape[dim] // parts).reshape((-1,) + (1,) * (len(shape) - dim - 1))

    level = one(*shards[0])
    for cut in shards[1:]:
        level = level * one(*cut)
    return level


def gaussian(own_key, shape, scale, limit, pieces=(), held_as=jnp.bfloat16):
    array = scale * jax.random.normal(own_key, shape, jnp.float32)
    if pieces:
        array = array * shard_levels(own_key, shape, pieces, -0.22, 0.18)
    return jnp.clip(array, -limit, limit).astype(held_as)


def setup_inputs(seed: int = 0) -> dict:
    key_of = jax.random.split(jax.random.key(seed), 7)
    return {
        "objects": gaussian(key_of[0], (2, 2, NY, NX), 0.7, 5.0, ((2, 4), (3, 8)), jnp.float32),
        "probe": gaussian(key_of[1], (2, WIN, WIN), 1.0, 6.0, (), jnp.float32),
        "prev_partial": gaussian(key_of[2], (N_ROW, N_COL, 2, WIN, WIN), 1.0, 6.0, ((0, 4), (1, 8)), jnp.float32),
        "offsets": with_ends(jax.random.randint(key_of[3], (N_ROW, N_COL, PAT, 2), 0, TILE + 2 * HALO - WIN + 1), jax.random.fold_in(key_of[3], 1), 0, TILE + 2 * HALO - WIN).astype(jnp.int32),
        "counts": with_ends(jax.random.randint(key_of[4], (N_ROW, N_COL), 0, PAT + 1), jax.random.fold_in(key_of[4], 1), 0, PAT).astype(jnp.int32),
        "amplitudes": jnp.clip(1.0 + 1.5 * jax.random.uniform(key_of[5], (N_ROW, N_COL, PAT, WIN, WIN), jnp.float32) ** shard_levels(key_of[5], (N_ROW, N_COL, PAT, WIN, WIN), ((0, 4), (1, 8)), -0.2, 0.2), 1.0, 2.5),
    }


OBJ_RATE = 0.1
PROBE_RATE = 0.3

def fresnel(n):
    index = jnp.arange(n, dtype=jnp.int32)
    freq = jnp.where(index < n // 2, index, index - n)
    square = (freq * freq).astype(jnp.float32)
    phase = jnp.pi * (square[:, None] + square[None, :]) / (4.0 * n)
    return (jnp.cos(phase), jnp.sin(phase))

def pattern_loss(ext, probe, offset, live, amp):
    zero = jnp.zeros((), jnp.int32)
    window = lax.dynamic_slice(ext, (zero, zero, offset[0].astype(jnp.int32), offset[1].astype(jnp.int32)), (2, 2, WIN, WIN))
    first = lax.complex(window[0, 0], window[0, 1])
    second = lax.complex(window[1, 0], window[1, 1])
    wave = lax.complex(probe[0], probe[1]) * first
    hre, him = fresnel(WIN)
    spectrum = jnp.fft.fft2(wave, norm='ortho') * lax.complex(hre, him)
    wave = jnp.fft.ifft2(spectrum, norm='ortho') * second
    far = jnp.fft.fft2(wave, norm='ortho')
    power = jnp.real(far) ** 2 + jnp.imag(far) ** 2
    return live * jnp.sum((jnp.sqrt(power + 1.0) - amp) ** 2)

def local_grads(ext, probe, offsets, count, amps):
    live = (jnp.arange(PAT, dtype=jnp.int32) < count).astype(jnp.float32)

    def total(ext_in, probe_in):
        losses = jax.vmap(pattern_loss, in_axes=(None, None, 0, 0, 0))(ext_in, probe_in, offsets, live, amps)
        return jnp.sum(losses)
    return jax.grad(total, argnums=(0, 1))(ext, probe)

def reference(objects, probe, prev_partial, offsets, counts, amplitudes):
    padded = jnp.pad(objects, ((0, 0), (0, 0), (HALO, HALO), (HALO, HALO)))
    side = TILE + 2 * HALO
    zero = jnp.zeros((), jnp.int32)

    def visit(grad_pad, index):
        tile_row = index // N_COL
        tile_col = index % N_COL
        top = (tile_row * TILE).astype(jnp.int32)
        left = (tile_col * TILE).astype(jnp.int32)
        ext = lax.dynamic_slice(padded, (zero, zero, top, left), (2, 2, side, side))
        grad_ext, grad_probe = local_grads(ext, probe, offsets[tile_row, tile_col], counts[tile_row, tile_col], amplitudes[tile_row, tile_col])
        old = lax.dynamic_slice(grad_pad, (zero, zero, top, left), (2, 2, side, side))
        grad_pad = lax.dynamic_update_slice(grad_pad, old + grad_ext, (zero, zero, top, left))
        return (grad_pad, grad_probe)
    start = jnp.zeros(padded.shape, jnp.float32)
    grad_pad, partials = lax.scan(visit, start, jnp.arange(N_ROW * N_COL, dtype=jnp.int32))
    grad = grad_pad[:, :, HALO:HALO + NY, HALO:HALO + NX]
    new_partial = partials.reshape(N_ROW, N_COL, 2, WIN, WIN)
    total = lax.optimization_barrier(jnp.sum(prev_partial, axis=(0, 1)))
    rate = PROBE_RATE / math.sqrt(N_ROW * N_COL)
    return (objects - OBJ_RATE * grad, probe - rate * total, new_partial)
```

```python
import functools
import math

import jax
import jax.numpy as jnp
import numpy as np
from jax import lax
from jax.experimental import pallas as pl
from jax.experimental.pallas import tpu as pltpu
from jax.sharding import PartitionSpec as P

HALO = 64
OBJ_RATE = 0.1
PROBE_RATE = 0.3
MESH = pl.DeviceIdType.MESH


def split(value):
    high = value.astype(jnp.bfloat16)
    low = (value - high.astype(jnp.float32)).astype(jnp.bfloat16)
    return high, low


def operator_table(n):
    index = np.arange(n)
    angle = 2.0 * np.pi * (np.outer(index, index) % n) / n
    dft = np.exp(-1j * angle) / np.sqrt(n)
    freq = np.where(index < n // 2, index, index - n).astype(np.float64)
    phase = np.exp(1j * np.pi * freq * freq / (4.0 * n))
    prop = np.conj(dft) @ (phase[:, None] * dft)
    tables = []
    for mat in (dft, prop):
        for part in (mat.real, mat.imag, -mat.imag):
            part = part.astype(np.float32)
            high = part.astype(jnp.bfloat16)
            low = (part - high.astype(np.float32)).astype(jnp.bfloat16)
            tables += [high, low]
    return np.stack(tables).reshape(2, 3, 2, n, n)


def dot(left, right):
    return jnp.dot(left, right, preferred_element_type=jnp.float32)


def cat(parts, axis):
    return jnp.concatenate(parts, axis=axis)


def sandwich(xr, xi, table, which, conj):
    re, im, neg = table.at[which, 0], table.at[which, 1], table.at[which, 2]
    if conj:
        im, neg = neg, im
    rh, rl, ih, il, nh, nl = (p[k] for p in (re, im, neg) for k in (0, 1))
    xrh, xrl = split(xr)
    xih, xil = split(xi)
    left = cat([xrh, xih, xrl, xil, xrh, xih], 1)
    tr = dot(left, cat([rh, nh, rh, nh, rl, nl], 0))
    ti = dot(left, cat([ih, rh, ih, rh, il, rl], 0))
    trh, trl = split(tr)
    tih, til = split(ti)
    right = cat([trh, tih, trl, til, trh, tih], 0)
    yr = dot(cat([rh, nh, rh, nh, rl, nl], 1), right)
    yi = dot(cat([ih, rh, ih, rh, il, rl], 1), right)
    return yr, yi


def kernel(
    rows, cols, offs, count, obj_hbm, prev_hbm, probe_hbm, probe_k_hbm, amp_hbm, table_hbm,
    out_obj, out_probe, out_part,
    obj, prev, probe, probe_piece, amp, table,
    my_off, off,
    ns_in, strip_mid, strip_edge, fold_far, far_mid, far_edge, msg_mid, msg_edge, got_mid, got_edge, z,
    gmsg_mid, gmsg_edge, gs_mid, gs_edge, acc_mid, acc_edge, ns_out, ns_back, new_mid, new_edge, part,
    buf1, sum1, buf2, newp,
    local_sem, out_sem, off_send, off_recv, ns_send, ns_recv, far_send, far_recv, msg_send, msg_recv,
    row_send, row_recv, col_send, col_recv, known,
):
    tile = obj.shape[2]
    mid_rows = tile - 2 * HALO
    wide = 2 * HALO
    row, col = lax.axis_index("row"), lax.axis_index("col")
    odd = lax.rem(col, 2)
    step = 1 - 2 * odd
    near = 1 - odd
    far = odd
    partner, other = col + step, col - step
    ahead, behind = col + 2 * step, col - 2 * step
    has_other = (other >= 0) & (other < cols)
    has_ahead = (ahead >= 0) & (ahead < cols)
    has_behind = (behind >= 0) & (behind < cols)
    has_north, has_south = row > 0, row < rows - 1
    always = row >= 0

    fetches = [
        pltpu.make_async_copy(src, dst, local_sem.at[k])
        for k, (src, dst) in enumerate(
            ((obj_hbm.at[0], obj.at[0]), (obj_hbm.at[1], obj.at[1]), (prev_hbm, prev),
             (probe_hbm, probe), (probe_k_hbm.at[row, col], probe_piece),
             (table_hbm, table), (amp_hbm, amp))
        )
    ]
    for fetch in fetches:
        fetch.start()

    barrier = pltpu.get_barrier_semaphore()

    def greet(sem, r, c):
        pl.semaphore_signal(sem, inc=1, device_id=(r, c), device_id_type=MESH)

    def flip(value, bit):
        return value + bit * (1 - 2 * lax.rem(value // bit, 2))

    bits = [1 << k for k in range(cols.bit_length() - 1)]
    expected = 0
    for t in range(1, rows):
        greet(barrier, lax.rem(row + t, rows), col)
        expected = expected + 1
    for ok, c in ((always, partner), (has_other, other), (has_ahead, ahead), (has_behind, behind)):
        @pl.when(ok)
        def _():
            greet(barrier, row, c)
        expected = expected + ok.astype(jnp.int32)
    for bit in bits[2:]:
        greet(barrier, row, flip(col, bit))
        expected = expected + 1

    top, left = offs[0], offs[1]
    my_off[0] = jnp.zeros((8, wide), jnp.int32) + top
    my_off[1] = jnp.zeros((8, wide), jnp.int32) + left

    lane = lax.broadcasted_iota(jnp.int32, (1, wide), 1)
    first = lane < HALO
    lane64 = jnp.where(first, lane, lane - HALO)
    line = lax.broadcasted_iota(jnp.int32, (wide, 1), 0)

    def swap(value):
        return pltpu.roll(value, HALO, 1)

    def turned(index, corner):
        return (index < corner - HALO) | (index >= corner + HALO)

    def pack(ref, slot):
        re, im = ref
        if slot == 0:
            return jnp.where(first, re[:, :wide], swap(im[:, :wide]))
        return jnp.where(first, swap(re[:, tile - wide :]), im[:, tile - wide :])

    def ends(value):
        return cat([value[:HALO], value[tile - HALO :]], 0)

    for s in range(2):
        fetches[s].wait()
        for slot in range(2):
            value = pack((obj[s, 0], obj[s, 1]), slot)
            strip_mid[slot, s] = value[HALO : tile - HALO]
            strip_edge[slot, s] = ends(value)
    fetches[3].wait()
    turn_rows = lax.rem(top + tile - HALO, tile)
    turn_cols = lax.rem(left + tile - HALO, tile)
    for k in range(2):
        probe[k] = pltpu.roll(pltpu.roll(probe[k], turn_rows, 0), turn_cols, 1)

    @pl.when(jnp.logical_not(has_other))
    def _():
        off[far] = jnp.full((2, 8, wide), HALO, jnp.int32)

    for s in range(2):
        @pl.when(jnp.logical_not(has_south))
        def _():
            ns_in[s, :, :HALO, :] = jnp.zeros((2, HALO, tile), jnp.float32)
            ns_back[s, :, HALO:, :] = jnp.zeros((2, HALO, tile), jnp.float32)

        @pl.when(jnp.logical_not(has_north))
        def _():
            ns_in[s, :, HALO:, :] = jnp.zeros((2, HALO, tile), jnp.float32)
            ns_back[s, :, :HALO, :] = jnp.zeros((2, HALO, tile), jnp.float32)

        @pl.when(jnp.logical_not(has_ahead))
        def _():
            far_mid[s] = jnp.zeros((mid_rows, wide), jnp.float32)
            far_edge[s] = jnp.zeros((wide, wide), jnp.float32)

        @pl.when(jnp.logical_not(has_behind))
        def _():
            gs_mid[far, s] = jnp.zeros((mid_rows, wide), jnp.float32)
            gs_edge[far, s] = jnp.zeros((wide, wide), jnp.float32)

    class Link:
        def __init__(self, src, dst, send_sem, recv_sem, device, ok, inbound):
            self.copy = pltpu.make_async_remote_copy(
                src_ref=src, dst_ref=dst, send_sem=send_sem, recv_sem=recv_sem,
                device_id=device, device_id_type=MESH)
            self.ok, self.inbound = ok, inbound

        def start(self):
            @pl.when(self.ok)
            def _():
                self.copy.start()

        def arrive(self):
            @pl.when(self.inbound)
            def _():
                self.copy.wait_recv()

        def sent(self):
            @pl.when(self.ok)
            def _():
                self.copy.wait_send()

    up, down = slice(0, HALO), slice(HALO, wide)
    off_near = Link(my_off, off.at[1 - near], off_send.at[0], off_recv.at[0], (row, partner), always, always)
    off_far = Link(my_off, off.at[1 - far], off_send.at[1], off_recv.at[1], (row, other), has_other, has_other)

    def ns_links(phase, s):
        if phase == 0:
            src_up, src_down, dst = obj.at[s, :, up, :], obj.at[s, :, tile - HALO :, :], ns_in
            to_up, to_down = (row - 1, has_north, has_south), (row + 1, has_south, has_north)
        else:
            src_up, src_down, dst = ns_out.at[s, :, up, :], ns_out.at[s, :, down, :], ns_back
            to_up, to_down = (row + 1, has_south, has_north), (row - 1, has_north, has_south)
        return [
            Link(src, dst.at[s, :, span, :], ns_send.at[phase, s, k], ns_recv.at[phase, s, k], (to[0], col), to[1], to[2])
            for k, (src, span, to) in enumerate(((src_up, up, to_up), (src_down, down, to_down)))
        ]

    ns = [[ns_links(phase, s) for s in range(2)] for phase in range(2)]
    MID, EDGE = 0, 1
    far_link = [
        [
            Link(strip_mid.at[far, s], far_mid.at[s], far_send.at[0, s, 0], far_recv.at[0, s, 0], (row, behind), has_behind, has_ahead),
            Link(fold_far.at[s], far_edge.at[s], far_send.at[0, s, 1], far_recv.at[0, s, 1], (row, behind), has_behind, has_ahead),
        ]
        for s in range(2)
    ]
    msg_link = [
        [
            Link(msg_mid.at[s], got_mid.at[s], msg_send.at[0, s, 0], msg_recv.at[0, s, 0], (row, partner), always, always),
            Link(msg_edge.at[s], got_edge.at[s], msg_send.at[0, s, 1], msg_recv.at[0, s, 1], (row, partner), always, always),
        ]
        for s in range(2)
    ]
    gmsg_link = [
        [
            Link(gmsg_mid.at[s], gs_mid.at[1 - near, s], msg_send.at[1, s, 0], msg_recv.at[1, s, 0], (row, partner), always, always),
            Link(gmsg_edge.at[s], gs_edge.at[1 - near, s], msg_send.at[1, s, 1], msg_recv.at[1, s, 1], (row, partner), always, always),
        ]
        for s in range(2)
    ]
    pass_link = [
        [
            Link(gs_mid.at[near, s], gs_mid.at[far, s], far_send.at[1, s, 0], far_recv.at[1, s, 0], (row, ahead), has_ahead, has_behind),
            Link(gs_edge.at[near, s], gs_edge.at[far, s], far_send.at[1, s, 1], far_recv.at[1, s, 1], (row, ahead), has_ahead, has_behind),
        ]
        for s in range(2)
    ]

    def row_copies(stage):
        made = []
        for t in range(1, rows):
            peer = lax.rem(row + t, rows)
            if stage == 0:
                src, dst = prev.at[peer], buf1.at[t - 1]
            else:
                src, dst = newp.at[row], newp.at[row]
            made.append(pltpu.make_async_remote_copy(
                src_ref=src, dst_ref=dst, send_sem=row_send.at[stage, t - 1],
                recv_sem=row_recv.at[stage, t - 1], device_id=(peer, col), device_id_type=MESH))
        return made

    def col_copies(stage):
        made = []
        for t in range(1, cols):
            peer = lax.rem(col + t, cols)
            if stage == 0:
                src, dst = sum1.at[peer], buf2.at[t - 1]
            else:
                src, dst = newp.at[row, col], newp.at[row, col]
            made.append(pltpu.make_async_remote_copy(
                src_ref=src, dst_ref=dst, send_sem=col_send.at[stage, t - 1],
                recv_sem=col_recv.at[stage, t - 1], device_id=(row, peer), device_id_type=MESH))
        return made

    fetches[2].wait()
    pl.semaphore_wait(barrier, expected)

    off_near.start()
    off_far.start()
    for s in range(2):
        for link in ns[0][s]:
            link.start()
        far_link[s][MID].start()
    rs_rows = row_copies(0)
    for copy in rs_rows:
        copy.start()
    for bit in bits:
        greet(known.at[0], row, flip(col, bit))

    off_near.arrive()
    off_far.arrive()
    near_off, far_off = off[near], off[far]
    near_top, near_left = near_off[0, :1], near_off[1, :1]
    far_top = far_off[0, :1]
    take_own = jnp.where(near == 0, near_left - HALO, HALO - near_left) > 0

    def fold(s):
        for link in ns[0][s]:
            link.arrive()
        packs = [pack((ns_in[s, 0], ns_in[s, 1]), slot) for slot in range(2)]
        far_pack = jnp.where(far == 0, packs[0], packs[1])
        near_pack = jnp.where(near == 0, packs[0], packs[1])
        fold_far[s] = jnp.where(turned(line, far_top), far_pack, strip_edge[far, s])
        far_link[s][EDGE].start()
        msg_edge[s] = jnp.where(turned(line, near_top), near_pack, strip_edge[near, s])

    def forward_mid(s):
        far_link[s][MID].arrive()
        msg_mid[s] = jnp.where(take_own, strip_mid[near, s], far_mid[s])
        msg_link[s][MID].start()

    def forward_edge(s):
        far_link[s][EDGE].arrive()
        msg_edge[s] = jnp.where(take_own, msg_edge[s], far_edge[s])
        msg_link[s][EDGE].start()

    for s in range(2):
        fold(s)
        forward_mid(s)
    for s in range(2):
        forward_edge(s)

    for wait_round, bit in enumerate(bits[1:]):
        pl.semaphore_wait(known.at[wait_round], len(bits))
        if wait_round + 1 < len(bits) - 1:
            for again in bits:
                greet(known.at[wait_round + 1], row, flip(col, again))

    def assemble(s):
        from_east, from_west = lane < left - HALO, lane >= left + HALO

        def columns(base, strip):
            turned_strip = swap(strip)
            for k in range(2):
                re_like, im_like = (strip, turned_strip) if k == 0 else (turned_strip, strip)
                head = jnp.where(from_east, re_like, base[k][:, :wide])
                tail = jnp.where(from_west, im_like, base[k][:, tile - wide :])
                yield cat([head, base[k][:, wide : tile - wide], tail], 1) if tile > 2 * wide else cat([head, tail], 1)

        msg_link[s][MID].arrive()
        for k, value in enumerate(columns([obj[s, p, HALO : tile - HALO, :] for p in range(2)], got_mid[s])):
            z[s, k, HALO : tile - HALO, :] = value
        msg_link[s][EDGE].arrive()
        base = [jnp.where(turned(line, top), ns_in[s, p], ends(obj[s, p])) for p in range(2)]
        for k, value in enumerate(columns(base, got_edge[s])):
            z[s, k, :HALO, :] = value[:HALO]
            z[s, k, tile - HALO :, :] = value[HALO:]

    def back(s, gre, gim):
        east = jnp.where(lane64 < left - HALO, pack((gre, gim), 0), 0.0)
        west = jnp.where(lane64 >= left, pack((gre, gim), 1), 0.0)
        value = jnp.where(left > HALO, east, west)
        gmsg_edge[s] = ends(value)
        gmsg_link[s][EDGE].start()
        gmsg_mid[s] = value[HALO : tile - HALO]
        gmsg_link[s][MID].start()
        away = turned(line, top)
        lanes = lax.broadcasted_iota(jnp.int32, (1, tile), 1)
        stay = jnp.logical_not((lanes < left - HALO) | (lanes >= left + tile - HALO))
        for k, grad in enumerate((gre, gim)):
            grad = jnp.where(stay, grad, 0.0)
            acc_mid[s, k] = grad[HALO : tile - HALO]
            edge = ends(grad)
            acc_edge[s, k] = jnp.where(away, 0.0, edge)
            ns_out[s, k] = jnp.where(away, edge, 0.0)

    fetches[5].wait()
    assemble(0)
    ar, ai = z[0, 0], z[0, 1]
    pr, pi = probe[0], probe[1]
    vr, vi = sandwich(pr * ar - pi * ai, pr * ai + pi * ar, table, 1, False)

    for copy in rs_rows:
        copy.wait_recv()
    total = prev[row]
    for t in range(1, rows):
        total = total + buf1[t - 1]
    sum1[...] = total
    rs_cols = col_copies(0)
    for copy in rs_cols:
        copy.start()

    assemble(1)
    br, bi = z[1, 0], z[1, 1]
    wr, wi = sandwich(vr * br - vi * bi, vr * bi + vi * br, table, 0, False)
    fetches[6].wait()
    live = jnp.where(count[0] > 0, 2.0, 0.0)
    scale = live * (1.0 - amp[...] / jnp.sqrt(wr * wr + wi * wi + 1.0))
    xr, xi = sandwich(scale * wr, scale * wi, table, 0, True)
    back(1, xr * vr + xi * vi, xi * vr - xr * vi)

    for copy in rs_cols:
        copy.wait_recv()
    fetches[4].wait()
    total = sum1[col]
    for t in range(1, cols):
        total = total + buf2[t - 1]
    rate = PROBE_RATE / math.sqrt(rows * cols)
    newp[row, col] = probe_piece[...] - rate * total
    ag_cols = col_copies(1)
    for copy in ag_cols:
        copy.start()

    ur, ui = sandwich(xr * br + xi * bi, xi * br - xr * bi, table, 1, True)
    back(0, ur * pr + ui * pi, ui * pr - ur * pi)

    for s in (1,):
        for piece in (EDGE, MID):
            gmsg_link[s][piece].arrive()
            pass_link[s][piece].start()

    for copy in ag_cols:
        copy.wait_recv()
    ag_rows = row_copies(1)
    for copy in ag_rows:
        copy.start()

    for s in (0,):
        for piece in (EDGE, MID):
            gmsg_link[s][piece].arrive()
            pass_link[s][piece].start()

    home_rows = lax.rem(tile + HALO - top, tile)
    home_cols = lax.rem(tile + HALO - left, tile)
    part[0] = pltpu.roll(pltpu.roll(ur * ar + ui * ai, home_rows, 0), home_cols, 1)
    part[1] = pltpu.roll(pltpu.roll(ui * ar - ur * ai, home_rows, 0), home_cols, 1)
    part_out = pltpu.make_async_copy(part, out_part, out_sem.at[0])
    part_out.start()

    head_off, tail_off = off[0], off[1]
    accept = (head_off[1, :1] > HALO, tail_off[1, :1] < HALO)
    corner = (head_off[0, :1], tail_off[0, :1])
    span = (slice(0, wide), slice(tile - wide, tile))

    def parts_of(slot, strip):
        if slot == 0:
            return jnp.where(first, strip, 0.0), jnp.where(first, swap(strip), 0.0)
        return jnp.where(first, 0.0, swap(strip)), jnp.where(first, 0.0, strip)

    def collect_edge(s):
        pass_link[s][EDGE].arrive()
        for slot in range(2):
            strip = jnp.where(accept[slot], gs_edge[slot, s], 0.0)
            moves = turned(line, corner[slot])
            for dst, kept in ((ns_out, jnp.where(moves, strip, 0.0)), (acc_edge, jnp.where(moves, 0.0, strip))):
                for k, value in enumerate(parts_of(slot, kept)):
                    dst[s, k, :, span[slot]] += value
        for link in ns[1][s]:
            link.start()

    writes = []

    def collect_mid(s):
        pass_link[s][MID].arrive()
        for slot in range(2):
            strip = jnp.where(accept[slot], gs_mid[slot, s], 0.0)
            for k, value in enumerate(parts_of(slot, strip)):
                acc_mid[s, k, :, span[slot]] += value
        for k in range(2):
            new_mid[s, k] = obj[s, k, HALO : tile - HALO, :] - OBJ_RATE * acc_mid[s, k]
        copy = pltpu.make_async_copy(new_mid.at[s], out_obj.at[s, :, HALO : tile - HALO, :], out_sem.at[1 + s])
        copy.start()
        writes.append(copy)

    def finish_edge(s):
        for link in ns[1][s]:
            link.arrive()
        for k in range(2):
            new_edge[s, k] = ends(obj[s, k]) - OBJ_RATE * (acc_edge[s, k] + ns_back[s, k])
        for k, (src, dst) in enumerate(((up, up), (down, slice(tile - HALO, tile)))):
            copy = pltpu.make_async_copy(new_edge.at[s, :, src, :], out_obj.at[s, :, dst, :], out_sem.at[3 + 2 * s + k])
            copy.start()
            writes.append(copy)

    collect_edge(1)
    collect_edge(0)
    collect_mid(1)
    collect_mid(0)
    finish_edge(1)
    for copy in ag_rows:
        copy.wait_recv()
    probe_out = pltpu.make_async_copy(newp, out_probe, out_sem.at[7])
    probe_out.start()
    finish_edge(0)

    off_near.sent()
    off_far.sent()
    for s in range(2):
        for phase in range(2):
            for link in ns[phase][s]:
                link.sent()
        for piece in range(2):
            for group in (far_link, msg_link, gmsg_link, pass_link):
                group[s][piece].sent()
    for copy in rs_rows + rs_cols + ag_cols + ag_rows:
        copy.wait_send()
    part_out.wait()
    for copy in writes:
        copy.wait()
    probe_out.wait()


def shards(rows, cols, objects, probe, prev_partial, offsets, counts, amplitudes):
    tile = objects.shape[2]
    win = probe.shape[-1]
    assert tile == win and cols % 2 == 0
    piece = (2 * win) // (rows * cols)
    split_shape = (rows, cols, piece, win)
    table = jnp.asarray(operator_table(win))
    f32 = jnp.float32
    smem = pl.BlockSpec(memory_space=pltpu.SMEM)
    anyspace = pl.BlockSpec(memory_space=pl.ANY)
    V = lambda *shape: pltpu.VMEM(shape, f32)
    mid, wide = tile - 2 * HALO, 2 * HALO
    dma = pltpu.SemaphoreType.DMA
    scratch = [
        V(2, 2, tile, tile), V(*split_shape), V(2, win, win), V(piece, win), V(win, win),
        pltpu.VMEM(table.shape, jnp.bfloat16),
        pltpu.VMEM((2, 8, wide), jnp.int32), pltpu.VMEM((2, 2, 8, wide), jnp.int32),
        V(2, 2, wide, tile), V(2, 2, mid, wide), V(2, 2, wide, wide), V(2, wide, wide),
        V(2, mid, wide), V(2, wide, wide), V(2, mid, wide), V(2, wide, wide), V(2, mid, wide), V(2, wide, wide),
        V(2, 2, tile, tile),
        V(2, mid, wide), V(2, wide, wide), V(2, 2, mid, wide), V(2, 2, wide, wide),
        V(2, 2, mid, tile), V(2, 2, wide, tile), V(2, 2, wide, tile), V(2, 2, wide, tile),
        V(2, 2, mid, tile), V(2, 2, wide, tile), V(2, win, win),
        V(max(rows - 1, 1), cols, piece, win), V(cols, piece, win),
        V(max(cols - 1, 1), piece, win), V(*split_shape),
        dma((7,)), dma((8,)), dma((2,)), dma((2,)), dma((2, 2, 2)), dma((2, 2, 2)),
        dma((2, 2, 2)), dma((2, 2, 2)), dma((2, 2, 2)), dma((2, 2, 2)),
        dma((2, max(rows - 1, 1))), dma((2, max(rows - 1, 1))),
        dma((2, max(cols - 1, 1))), dma((2, max(cols - 1, 1))),
        pltpu.SemaphoreType.REGULAR((max(cols.bit_length() - 2, 1),)),
    ]
    new_obj, new_probe, part = pl.pallas_call(
        functools.partial(kernel, rows, cols),
        out_shape=(
            jax.ShapeDtypeStruct(objects.shape, f32),
            jax.ShapeDtypeStruct(split_shape, f32),
            jax.ShapeDtypeStruct(probe.shape, f32),
        ),
        in_specs=[smem, smem] + [anyspace] * 6,
        out_specs=(anyspace, anyspace, anyspace),
        scratch_shapes=scratch,
        compiler_params=pltpu.CompilerParams(
            collective_id=0, has_side_effects=True, vmem_limit_bytes=56 * 2**20
        ),
    )(
        offsets.reshape(2), counts.reshape(1), objects, prev_partial.reshape(split_shape),
        probe, probe.reshape(split_shape), amplitudes.reshape(win, win), table,
    )
    return new_obj, new_probe.reshape(probe.shape), part[None, None]


def solution(mesh):
    in_specs = (
        P(None, None, "row", "col"),
        P(),
        P("row", "col", None, None, None),
        P("row", "col", None, None),
        P("row", "col"),
        P("row", "col", None, None, None),
    )
    out_specs = (P(None, None, "row", "col"), P(), P("row", "col", None, None, None))
    body = functools.partial(shards, mesh.shape["row"], mesh.shape["col"])
    return jax.shard_map(body, mesh=mesh, in_specs=in_specs, out_specs=out_specs, check_vma=False)
```

```python
import functools
import math

import jax
import jax.numpy as jnp
import numpy as np
from jax import lax
from jax.experimental import pallas as pl
from jax.experimental.pallas import tpu as pltpu
from jax.sharding import PartitionSpec as P

HALO = 64
OBJ_RATE = 0.1
PROBE_RATE = 0.3
MESH = pl.DeviceIdType.MESH


def split(value):
    high = value.astype(jnp.bfloat16)
    low = (value - high.astype(jnp.float32)).astype(jnp.bfloat16)
    return high, low


def operator_table(n):
    half = n // 2
    index = np.arange(n)
    dft = np.exp(-2j * np.pi * (np.outer(index, index) % n) / n) / np.sqrt(n)
    freq = np.where(index < half, index, index - n).astype(np.float64)
    phase = np.exp(1j * np.pi * freq * freq / (4.0 * n))
    prop = np.conj(dft) @ (phase[:, None] * dft)
    near, far = prop[:half, :half], prop[:half, half:]
    tables = []
    for mat in (dft[0::2, :half], dft[1::2, :half], (near + far) / 2, (near - far) / 2):
        right = np.block([[mat.real.T, mat.imag.T], [-mat.imag.T, mat.real.T]]).astype(np.float32)
        for part in (right, right.T):
            high = part.astype(jnp.bfloat16)
            tables += [high, (part - high.astype(np.float32)).astype(jnp.bfloat16)]
    return np.stack(tables).reshape(2, 2, 2, 2, n, n)


def dot(left, right):
    return jnp.dot(left, right, preferred_element_type=jnp.float32)


def cat(parts, axis):
    return jnp.concatenate(parts, axis=axis)


def times(data, table, which, side, flip):
    kind = int(flip if side else not flip)
    out = []
    for k in range(2):
        high, low = table[which, k, kind, 0], table[which, k, kind, 1]
        dh, dl = split(data[k])
        if side:
            out.append(dot(cat([dh, dl, dh], 1), cat([high, high, low], 0)))
        else:
            out.append(dot(cat([high, high, low], 1), cat([dh, dl, dh], 0)))
    return out


def halves(value, axis):
    half = value.shape[axis] // 2
    return (value[:half], value[half:]) if axis == 0 else (value[:, :half], value[:, half:])


def transform(re, im, table, which, axis, merge, divide, flip):
    if divide:
        parts = [halves(v, axis) for v in (re, im)]
        data = [cat([a + b for a, b in parts], axis), cat([a - b for a, b in parts], axis)]
    else:
        parts = [halves(v, axis) for v in (re, im)]
        data = [cat([p[0] for p in parts], axis), cat([p[1] for p in parts], axis)]
    even, odd = [halves(v, axis) for v in times(data, table, which, axis, flip)]
    if merge:
        return [cat([a + b, a - b], axis) for a, b in zip(even, odd)]
    return [cat([a, b], axis) for a, b in zip(even, odd)]


def sandwich(xr, xi, table, which, conj):
    divide = which == 1 or not conj
    merge = which == 1 or conj
    tr, ti = transform(xr, xi, table, which, 1, merge, divide, conj)
    return transform(tr, ti, table, which, 0, merge, divide, conj)


def kernel(
    rows, cols, offs, count, obj_hbm, prev_hbm, probe_hbm, probe_k_hbm, amp_hbm, table_hbm,
    out_obj, out_probe, out_part,
    obj, prev, probe, probe_piece, amp, table,
    my_off, off,
    ns_in, strip_mid, strip_edge, fold_far, far_mid, far_edge, msg_mid, msg_edge, got_mid, got_edge, z,
    gmsg_mid, gmsg_edge, gs_mid, gs_edge, acc_mid, acc_edge, ns_out, ns_back,
    buf1, buf2,
    local_sem, off_send, off_recv, ns_send, ns_recv, far_send, far_recv, msg_send, msg_recv,
    row_send, row_recv, col_send, col_recv, known,
):
    tile = obj.shape[2]
    mid_rows = tile - 2 * HALO
    wide = 2 * HALO
    row, col = lax.axis_index("row"), lax.axis_index("col")
    odd = lax.rem(col, 2)
    step = 1 - 2 * odd
    near = 1 - odd
    far = odd
    partner, other = col + step, col - step
    ahead, behind = col + 2 * step, col - 2 * step
    has_other = (other >= 0) & (other < cols)
    has_ahead = (ahead >= 0) & (ahead < cols)
    has_behind = (behind >= 0) & (behind < cols)
    has_north, has_south = row > 0, row < rows - 1
    always = row >= 0

    def flip(value, bit):
        return value + bit * (1 - 2 * lax.rem(value // bit, 2))

    row_bits = [1 << k for k in range(rows.bit_length() - 1)]
    base, length, row_down, row_keep = 0, rows, [], []
    for k, bit in enumerate(row_bits):
        length = length // 2
        upper = lax.rem(row // bit, 2)
        keep, give = base + upper * length, base + (1 - upper) * length
        landing = buf1.at[pl.ds(rows - 2 * length, length)]
        row_down.append(pltpu.make_async_remote_copy(
            src_ref=prev.at[pl.ds(give, length)], dst_ref=landing, send_sem=row_send.at[0, k],
            recv_sem=row_recv.at[0, k], device_id=(flip(row, bit), col), device_id_type=MESH))
        row_keep.append((keep, length, landing))
        base = keep
    slot = base
    row_up = []
    for k, bit in enumerate(reversed(row_bits)):
        here = out_probe.at[pl.ds(base, length)]
        row_up.append(pltpu.make_async_remote_copy(
            src_ref=here, dst_ref=here, send_sem=row_send.at[1, k],
            recv_sem=row_recv.at[1, k], device_id=(flip(row, bit), col), device_id_type=MESH))
        base = base - length * lax.rem(row // bit, 2)
        length = 2 * length

    fetches = [
        pltpu.make_async_copy(src, dst, local_sem.at[k])
        for k, (src, dst) in enumerate(
            ((obj_hbm.at[0], obj.at[0]), (obj_hbm.at[1], obj.at[1]), (prev_hbm, prev),
             (probe_hbm, probe), (probe_k_hbm.at[slot, col], probe_piece),
             (table_hbm, table), (amp_hbm, amp))
        )
    ]
    for fetch in fetches:
        fetch.start()

    barrier = pltpu.get_barrier_semaphore()

    def greet(sem, r, c):
        pl.semaphore_signal(sem, inc=1, device_id=(r, c), device_id_type=MESH)

    bits = [1 << k for k in range(cols.bit_length() - 1)]
    expected = 0
    for t in range(1, rows):
        greet(barrier, lax.rem(row + t, rows), col)
        expected = expected + 1
    for ok, c in ((always, partner), (has_other, other), (has_ahead, ahead), (has_behind, behind)):
        @pl.when(ok)
        def _():
            greet(barrier, row, c)
        expected = expected + ok.astype(jnp.int32)
    for bit in bits[2:]:
        greet(barrier, row, flip(col, bit))
        expected = expected + 1

    top, left = offs[0], offs[1]
    my_off[0] = jnp.zeros((8, wide), jnp.int32) + top
    my_off[1] = jnp.zeros((8, wide), jnp.int32) + left

    lane = lax.broadcasted_iota(jnp.int32, (1, wide), 1)
    first = lane < HALO
    lane64 = jnp.where(first, lane, lane - HALO)
    line = lax.broadcasted_iota(jnp.int32, (wide, 1), 0)

    def swap(value):
        return pltpu.roll(value, HALO, 1)

    def turned(index, corner):
        return (index < corner - HALO) | (index >= corner + HALO)

    def pack(ref, slot):
        re, im = ref
        if slot == 0:
            return jnp.where(first, re[:, :wide], swap(im[:, :wide]))
        return jnp.where(first, swap(re[:, tile - wide :]), im[:, tile - wide :])

    def ends(value):
        return cat([value[:HALO], value[tile - HALO :]], 0)

    for s in range(2):
        fetches[s].wait()
        for side in range(2):
            value = pack((obj[s, 0], obj[s, 1]), side)
            strip_mid[side, s] = value[HALO : tile - HALO]
            strip_edge[side, s] = ends(value)
    fetches[3].wait()
    turn_rows = lax.rem(top + tile - HALO, tile)
    turn_cols = lax.rem(left + tile - HALO, tile)
    for k in range(2):
        probe[k] = pltpu.roll(pltpu.roll(probe[k], turn_rows, 0), turn_cols, 1)

    fetches[6].wait()
    count_half = tile // 2

    def order(axis):
        target = lax.broadcasted_iota(jnp.int32, (tile, tile), axis)
        source = lax.broadcasted_iota(jnp.int32, (tile, tile), 1 - axis)
        target = jnp.where(target < count_half, 2 * target, 2 * (target - count_half) + 1)
        return (source == target).astype(jnp.float32).astype(jnp.bfloat16)

    ordered = dot(cat([order(0), order(0)], 1), cat(split(amp[...]), 0))
    amp[...] = dot(cat(split(ordered), 1), cat([order(1), order(1)], 0))

    @pl.when(jnp.logical_not(has_other))
    def _():
        off[far] = jnp.full((2, 8, wide), HALO, jnp.int32)

    for s in range(2):
        @pl.when(jnp.logical_not(has_south))
        def _():
            ns_in[s, :, :HALO, :] = jnp.zeros((2, HALO, tile), jnp.float32)
            ns_back[s, :, HALO:, :] = jnp.zeros((2, HALO, tile), jnp.float32)

        @pl.when(jnp.logical_not(has_north))
        def _():
            ns_in[s, :, HALO:, :] = jnp.zeros((2, HALO, tile), jnp.float32)
            ns_back[s, :, :HALO, :] = jnp.zeros((2, HALO, tile), jnp.float32)

        @pl.when(jnp.logical_not(has_ahead))
        def _():
            far_mid[s] = jnp.zeros((mid_rows, wide), jnp.float32)
            far_edge[s] = jnp.zeros((wide, wide), jnp.float32)

        @pl.when(jnp.logical_not(has_behind))
        def _():
            gs_mid[far, s] = jnp.zeros((mid_rows, wide), jnp.float32)
            gs_edge[far, s] = jnp.zeros((wide, wide), jnp.float32)

    class Link:
        def __init__(self, src, dst, send_sem, recv_sem, device, ok, inbound):
            self.copy = pltpu.make_async_remote_copy(
                src_ref=src, dst_ref=dst, send_sem=send_sem, recv_sem=recv_sem,
                device_id=device, device_id_type=MESH)
            self.ok, self.inbound = ok, inbound

        def start(self):
            @pl.when(self.ok)
            def _():
                self.copy.start()

        def arrive(self):
            @pl.when(self.inbound)
            def _():
                self.copy.wait_recv()

        def sent(self):
            @pl.when(self.ok)
            def _():
                self.copy.wait_send()

    up, down = slice(0, HALO), slice(HALO, wide)
    off_near = Link(my_off, off.at[1 - near], off_send.at[0], off_recv.at[0], (row, partner), always, always)
    off_far = Link(my_off, off.at[1 - far], off_send.at[1], off_recv.at[1], (row, other), has_other, has_other)

    def ns_links(phase, s):
        if phase == 0:
            src_up, src_down, dst = obj.at[s, :, up, :], obj.at[s, :, tile - HALO :, :], ns_in
            to_up, to_down = (row - 1, has_north, has_south), (row + 1, has_south, has_north)
        else:
            src_up, src_down, dst = ns_out.at[s, :, up, :], ns_out.at[s, :, down, :], ns_back
            to_up, to_down = (row + 1, has_south, has_north), (row - 1, has_north, has_south)
        return [
            Link(src, dst.at[s, :, span, :], ns_send.at[phase, s, k], ns_recv.at[phase, s, k], (to[0], col), to[1], to[2])
            for k, (src, span, to) in enumerate(((src_up, up, to_up), (src_down, down, to_down)))
        ]

    ns = [[ns_links(phase, s) for s in range(2)] for phase in range(2)]
    MID, EDGE = 0, 1
    far_link = [
        [
            Link(strip_mid.at[far, s], far_mid.at[s], far_send.at[0, s, 0], far_recv.at[0, s, 0], (row, behind), has_behind, has_ahead),
            Link(fold_far.at[s], far_edge.at[s], far_send.at[0, s, 1], far_recv.at[0, s, 1], (row, behind), has_behind, has_ahead),
        ]
        for s in range(2)
    ]
    msg_link = [
        [
            Link(msg_mid.at[s], got_mid.at[s], msg_send.at[0, s, 0], msg_recv.at[0, s, 0], (row, partner), always, always),
            Link(msg_edge.at[s], got_edge.at[s], msg_send.at[0, s, 1], msg_recv.at[0, s, 1], (row, partner), always, always),
        ]
        for s in range(2)
    ]
    gmsg_link = [
        [
            Link(gmsg_mid.at[s], gs_mid.at[1 - near, s], msg_send.at[1, s, 0], msg_recv.at[1, s, 0], (row, partner), always, always),
            Link(gmsg_edge.at[s], gs_edge.at[1 - near, s], msg_send.at[1, s, 1], msg_recv.at[1, s, 1], (row, partner), always, always),
        ]
        for s in range(2)
    ]
    pass_link = [
        [
            Link(gs_mid.at[near, s], gs_mid.at[far, s], far_send.at[1, s, 0], far_recv.at[1, s, 0], (row, ahead), has_ahead, has_behind),
            Link(gs_edge.at[near, s], gs_edge.at[far, s], far_send.at[1, s, 1], far_recv.at[1, s, 1], (row, ahead), has_ahead, has_behind),
        ]
        for s in range(2)
    ]

    def add_rows(k):
        keep, count_rows, landing = row_keep[k]
        row_down[k].wait_recv()
        prev[pl.ds(keep, count_rows)] += landing[...]

    def col_copies(stage):
        made = []
        for t in range(1, cols):
            peer = lax.rem(col + t, cols)
            if stage == 0:
                src, dst = prev.at[slot, peer], buf2.at[t - 1]
            else:
                src, dst = out_probe.at[slot, col], out_probe.at[slot, col]
            made.append(pltpu.make_async_remote_copy(
                src_ref=src, dst_ref=dst, send_sem=col_send.at[stage, t - 1],
                recv_sem=col_recv.at[stage, t - 1], device_id=(row, peer), device_id_type=MESH))
        return made

    fetches[2].wait()
    pl.semaphore_wait(barrier, expected)

    off_near.start()
    off_far.start()
    row_down[0].start()
    for s in range(2):
        for link in ns[0][s]:
            link.start()
        far_link[s][MID].start()
    for bit in bits:
        greet(known.at[0], row, flip(col, bit))

    off_near.arrive()
    off_far.arrive()
    near_off, far_off = off[near], off[far]
    near_top, near_left = near_off[0, :1], near_off[1, :1]
    far_top = far_off[0, :1]
    take_own = jnp.where(near == 0, near_left - HALO, HALO - near_left) > 0

    def fold(s):
        for link in ns[0][s]:
            link.arrive()
        packs = [pack((ns_in[s, 0], ns_in[s, 1]), slot) for slot in range(2)]
        far_pack = jnp.where(far == 0, packs[0], packs[1])
        near_pack = jnp.where(near == 0, packs[0], packs[1])
        fold_far[s] = jnp.where(turned(line, far_top), far_pack, strip_edge[far, s])
        far_link[s][EDGE].start()
        msg_edge[s] = jnp.where(turned(line, near_top), near_pack, strip_edge[near, s])

    def forward_mid(s):
        far_link[s][MID].arrive()
        msg_mid[s] = jnp.where(take_own, strip_mid[near, s], far_mid[s])
        msg_link[s][MID].start()

    def forward_edge(s):
        far_link[s][EDGE].arrive()
        msg_edge[s] = jnp.where(take_own, msg_edge[s], far_edge[s])
        msg_link[s][EDGE].start()

    fold(0)
    forward_mid(0)
    add_rows(0)
    for k in range(1, len(row_bits)):
        row_down[k].start()
        if k + 1 < len(row_bits):
            add_rows(k)
    fold(1)
    forward_mid(1)
    forward_edge(0)
    forward_edge(1)

    for wait_round, bit in enumerate(bits[1:]):
        pl.semaphore_wait(known.at[wait_round], len(bits))
        if wait_round + 1 < len(bits) - 1:
            for again in bits:
                greet(known.at[wait_round + 1], row, flip(col, again))

    def assemble(s):
        from_east, from_west = lane < left - HALO, lane >= left + HALO

        def columns(base, strip):
            turned_strip = swap(strip)
            for k in range(2):
                re_like, im_like = (strip, turned_strip) if k == 0 else (turned_strip, strip)
                head = jnp.where(from_east, re_like, base[k][:, :wide])
                tail = jnp.where(from_west, im_like, base[k][:, tile - wide :])
                yield cat([head, base[k][:, wide : tile - wide], tail], 1) if tile > 2 * wide else cat([head, tail], 1)

        msg_link[s][MID].arrive()
        for k, value in enumerate(columns([obj[s, p, HALO : tile - HALO, :] for p in range(2)], got_mid[s])):
            z[s, k, HALO : tile - HALO, :] = value
        msg_link[s][EDGE].arrive()
        base = [jnp.where(turned(line, top), ns_in[s, p], ends(obj[s, p])) for p in range(2)]
        for k, value in enumerate(columns(base, got_edge[s])):
            z[s, k, :HALO, :] = value[:HALO]
            z[s, k, tile - HALO :, :] = value[HALO:]

    def back(s, gre, gim):
        east = jnp.where(lane64 < left - HALO, pack((gre, gim), 0), 0.0)
        west = jnp.where(lane64 >= left, pack((gre, gim), 1), 0.0)
        value = jnp.where(left > HALO, east, west)
        gmsg_edge[s] = ends(value)
        gmsg_link[s][EDGE].start()
        gmsg_mid[s] = value[HALO : tile - HALO]
        gmsg_link[s][MID].start()
        away = turned(line, top)
        lanes = lax.broadcasted_iota(jnp.int32, (1, tile), 1)
        stay = jnp.logical_not((lanes < left - HALO) | (lanes >= left + tile - HALO))
        for k, grad in enumerate((gre, gim)):
            grad = jnp.where(stay, grad, 0.0)
            acc_mid[s, k] = grad[HALO : tile - HALO]
            edge = ends(grad)
            acc_edge[s, k] = jnp.where(away, 0.0, edge)
            ns_out[s, k] = jnp.where(away, edge, 0.0)

    if len(row_bits) > 1:
        add_rows(len(row_bits) - 1)
    rs_cols = col_copies(0)
    for copy in rs_cols:
        copy.start()

    fetches[5].wait()
    assemble(0)
    ar, ai = z[0, 0], z[0, 1]
    pr, pi = probe[0], probe[1]
    vr, vi = sandwich(pr * ar - pi * ai, pr * ai + pi * ar, table, 1, False)

    assemble(1)
    br, bi = z[1, 0], z[1, 1]
    wr, wi = sandwich(vr * br - vi * bi, vr * bi + vi * br, table, 0, False)
    for copy in rs_cols:
        copy.wait_recv()
    fetches[4].wait()
    total = prev[slot, col]
    for t in range(1, cols):
        total = total + buf2[t - 1]
    rate = PROBE_RATE / math.sqrt(rows * cols)
    out_probe[slot, col] = probe_piece[...] - rate * total
    ag_cols = col_copies(1)
    for copy in ag_cols:
        copy.start()

    live = jnp.where(count[0] > 0, 2.0, 0.0)
    scale = live - (live * amp[...]) * lax.rsqrt(wr * wr + wi * wi + 1.0)
    xr, xi = sandwich(scale * wr, scale * wi, table, 0, True)
    back(1, xr * vr + xi * vi, xi * vr - xr * vi)

    ur, ui = sandwich(xr * br + xi * bi, xi * br - xr * bi, table, 1, True)
    back(0, ur * pr + ui * pi, ui * pr - ur * pi)

    for s in (1,):
        for piece in (EDGE, MID):
            gmsg_link[s][piece].arrive()
            pass_link[s][piece].start()

    for copy in ag_cols:
        copy.wait_recv()
    row_up[0].start()

    for s in (0,):
        for piece in (EDGE, MID):
            gmsg_link[s][piece].arrive()
            pass_link[s][piece].start()

    home_rows = lax.rem(tile + HALO - top, tile)
    home_cols = lax.rem(tile + HALO - left, tile)
    out_part[0] = pltpu.roll(pltpu.roll(ur * ar + ui * ai, home_rows, 0), home_cols, 1)
    out_part[1] = pltpu.roll(pltpu.roll(ui * ar - ur * ai, home_rows, 0), home_cols, 1)

    head_off, tail_off = off[0], off[1]
    accept = (head_off[1, :1] > HALO, tail_off[1, :1] < HALO)
    corner = (head_off[0, :1], tail_off[0, :1])
    span = (slice(0, wide), slice(tile - wide, tile))

    def parts_of(slot, strip):
        if slot == 0:
            return jnp.where(first, strip, 0.0), jnp.where(first, swap(strip), 0.0)
        return jnp.where(first, 0.0, swap(strip)), jnp.where(first, 0.0, strip)

    def collect_edge(s):
        pass_link[s][EDGE].arrive()
        for slot in range(2):
            strip = jnp.where(accept[slot], gs_edge[slot, s], 0.0)
            moves = turned(line, corner[slot])
            for dst, kept in ((ns_out, jnp.where(moves, strip, 0.0)), (acc_edge, jnp.where(moves, 0.0, strip))):
                for k, value in enumerate(parts_of(slot, kept)):
                    dst[s, k, :, span[slot]] += value
        for link in ns[1][s]:
            link.start()

    def collect_mid(s):
        pass_link[s][MID].arrive()
        for slot in range(2):
            strip = jnp.where(accept[slot], gs_mid[slot, s], 0.0)
            for k, value in enumerate(parts_of(slot, strip)):
                acc_mid[s, k, :, span[slot]] += value
        for k in range(2):
            out_obj[s, k, HALO : tile - HALO, :] = obj[s, k, HALO : tile - HALO, :] - OBJ_RATE * acc_mid[s, k]

    def finish_edge(s):
        for link in ns[1][s]:
            link.arrive()
        for k in range(2):
            value = ends(obj[s, k]) - OBJ_RATE * (acc_edge[s, k] + ns_back[s, k])
            out_obj[s, k, :HALO, :] = value[:HALO]
            out_obj[s, k, tile - HALO :, :] = value[HALO:]

    collect_edge(1)
    collect_edge(0)
    collect_mid(1)
    collect_mid(0)
    for k in range(1, len(row_bits)):
        row_up[k - 1].wait_recv()
        row_up[k].start()
    finish_edge(1)
    row_up[-1].wait_recv()
    finish_edge(0)

    off_near.sent()
    off_far.sent()
    for s in range(2):
        for phase in range(2):
            for link in ns[phase][s]:
                link.sent()
        for piece in range(2):
            for group in (far_link, msg_link, gmsg_link, pass_link):
                group[s][piece].sent()
    for copy in row_down + rs_cols + ag_cols + row_up:
        copy.wait_send()


def store(obj, probe, part, out_obj, out_probe, out_part, sem):
    copies = [
        pltpu.make_async_copy(src, dst, sem.at[k])
        for k, (src, dst) in enumerate(((obj, out_obj), (probe, out_probe), (part, out_part)))
    ]
    for copy in copies:
        copy.start()
    for copy in copies:
        copy.wait()


def shards(rows, cols, objects, probe, prev_partial, offsets, counts, amplitudes):
    tile = objects.shape[2]
    win = probe.shape[-1]
    assert tile == win and cols % 2 == 0
    piece = (2 * win) // (rows * cols)
    split_shape = (rows, cols, piece, win)
    table = jnp.asarray(operator_table(win))
    f32 = jnp.float32
    smem = pl.BlockSpec(memory_space=pltpu.SMEM)
    anyspace = pl.BlockSpec(memory_space=pl.ANY)
    vmem = pl.BlockSpec(memory_space=pltpu.VMEM)
    V = lambda *shape: pltpu.VMEM(shape, f32)
    mid, wide = tile - 2 * HALO, 2 * HALO
    dma = pltpu.SemaphoreType.DMA
    scratch = [
        V(2, 2, tile, tile), V(*split_shape), V(2, win, win), V(piece, win), V(win, win),
        pltpu.VMEM(table.shape, jnp.bfloat16),
        pltpu.VMEM((2, 8, wide), jnp.int32), pltpu.VMEM((2, 2, 8, wide), jnp.int32),
        V(2, 2, wide, tile), V(2, 2, mid, wide), V(2, 2, wide, wide), V(2, wide, wide),
        V(2, mid, wide), V(2, wide, wide), V(2, mid, wide), V(2, wide, wide), V(2, mid, wide), V(2, wide, wide),
        V(2, 2, tile, tile),
        V(2, mid, wide), V(2, wide, wide), V(2, 2, mid, wide), V(2, 2, wide, wide),
        V(2, 2, mid, tile), V(2, 2, wide, tile), V(2, 2, wide, tile), V(2, 2, wide, tile),
        V(max(rows - 1, 1), cols, piece, win), V(max(cols - 1, 1), piece, win),
        dma((7,)), dma((2,)), dma((2,)), dma((2, 2, 2)), dma((2, 2, 2)),
        dma((2, 2, 2)), dma((2, 2, 2)), dma((2, 2, 2)), dma((2, 2, 2)),
        dma((2, max(rows - 1, 1))), dma((2, max(rows - 1, 1))),
        dma((2, max(cols - 1, 1))), dma((2, max(cols - 1, 1))),
        pltpu.SemaphoreType.REGULAR((max(cols.bit_length() - 2, 1),)),
    ]
    results = pl.pallas_call(
        functools.partial(kernel, rows, cols),
        out_shape=(
            pltpu.VMEM(objects.shape, f32), pltpu.VMEM(split_shape, f32), pltpu.VMEM(probe.shape, f32),
        ),
        in_specs=[smem, smem] + [anyspace] * 6,
        out_specs=(vmem, vmem, vmem),
        scratch_shapes=scratch,
        compiler_params=pltpu.CompilerParams(
            collective_id=0, has_side_effects=True, vmem_limit_bytes=56 * 2**20
        ),
    )(
        offsets.reshape(2), counts.reshape(1), objects, prev_partial.reshape(split_shape),
        probe, probe.reshape(split_shape), amplitudes.reshape(win, win), table,
    )
    new_obj, new_probe, part = pl.pallas_call(
        store,
        out_shape=tuple(jax.ShapeDtypeStruct(v.shape, f32) for v in results),
        in_specs=[vmem] * 3,
        out_specs=(pl.BlockSpec(memory_space=pltpu.HBM),) * 3,
        scratch_shapes=[dma((3,))],
    )(*[pltpu.with_memory_space_constraint(v, pltpu.VMEM) for v in results])
    return new_obj, new_probe.reshape(probe.shape), part[None, None]


def solution(mesh):
    in_specs = (
        P(None, None, "row", "col"),
        P(),
        P("row", "col", None, None, None),
        P("row", "col", None, None),
        P("row", "col"),
        P("row", "col", None, None, None),
    )
    out_specs = (P(None, None, "row", "col"), P(), P("row", "col", None, None, None))
    body = functools.partial(shards, mesh.shape["row"], mesh.shape["col"])
    return jax.shard_map(body, mesh=mesh, in_specs=in_specs, out_specs=out_specs, check_vma=False)
```

```python
import functools
import math

import jax
import jax.numpy as jnp
import numpy as np
from jax import lax
from jax.experimental import pallas as pl
from jax.experimental.pallas import tpu as pltpu
from jax.sharding import PartitionSpec as P

HALO = 64
OBJ_RATE = 0.1
PROBE_RATE = 0.3
MESH = pl.DeviceIdType.MESH


def split(value):
    high = value.astype(jnp.bfloat16)
    low = (value - high.astype(jnp.float32)).astype(jnp.bfloat16)
    return high, low


def operator_table(n):
    half = n // 2
    index = np.arange(n)
    dft = np.exp(-2j * np.pi * (np.outer(index, index) % n) / n) / np.sqrt(n)
    freq = np.where(index < half, index, index - n).astype(np.float64)
    phase = np.exp(1j * np.pi * freq * freq / (4.0 * n))
    prop = np.conj(dft) @ (phase[:, None] * dft)
    near, far = prop[:half, :half], prop[:half, half:]
    tables = []
    for mat in (dft[0::2, :half], dft[1::2, :half], (near + far) / 2, (near - far) / 2):
        right = np.block([[mat.real.T, mat.imag.T], [-mat.imag.T, mat.real.T]]).astype(np.float32)
        for part in (right, right.T):
            high = part.astype(jnp.bfloat16)
            tables += [high, (part - high.astype(np.float32)).astype(jnp.bfloat16)]
    return np.stack(tables).reshape(2, 2, 2, 2, n, n)


def dot(left, right):
    return jnp.dot(left, right, preferred_element_type=jnp.float32)


def cat(parts, axis):
    return jnp.concatenate(parts, axis=axis)


def times(data, table, which, side, flip):
    kind = int(flip if side else not flip)
    out = []
    for k in range(2):
        high, low = table[which, k, kind, 0], table[which, k, kind, 1]
        dh, dl = split(data[k])
        if side:
            out.append(dot(cat([dh, dl, dh], 1), cat([high, high, low], 0)))
        else:
            out.append(dot(cat([high, high, low], 1), cat([dh, dl, dh], 0)))
    return out


def halves(value, axis):
    half = value.shape[axis] // 2
    return (value[:half], value[half:]) if axis == 0 else (value[:, :half], value[:, half:])


def transform(re, im, table, which, axis, merge, divide, flip):
    if divide:
        parts = [halves(v, axis) for v in (re, im)]
        data = [cat([a + b for a, b in parts], axis), cat([a - b for a, b in parts], axis)]
    else:
        parts = [halves(v, axis) for v in (re, im)]
        data = [cat([p[0] for p in parts], axis), cat([p[1] for p in parts], axis)]
    even, odd = [halves(v, axis) for v in times(data, table, which, axis, flip)]
    if merge:
        return [cat([a + b, a - b], axis) for a, b in zip(even, odd)]
    return [cat([a, b], axis) for a, b in zip(even, odd)]


def sandwich(xr, xi, table, which, conj):
    divide = which == 1 or not conj
    merge = which == 1 or conj
    tr, ti = transform(xr, xi, table, which, 1, merge, divide, conj)
    return transform(tr, ti, table, which, 0, merge, divide, conj)


def kernel(
    rows, cols, offs, count, obj_hbm, prev_hbm, probe_hbm, probe_k_hbm, amp_hbm, table_hbm,
    out_obj, out_probe, out_part,
    obj, prev, probe, probe_piece, amp, table,
    my_off, off,
    ns_in, strip_mid, strip_edge, fold_far, far_mid, far_edge, msg_mid, msg_edge, got_mid, got_edge, z,
    gmsg_mid, gmsg_edge, gs_mid, gs_edge, acc_mid, acc_edge, ns_out, ns_back,
    buf1, buf2,
    local_sem, off_send, off_recv, ns_send, ns_recv, far_send, far_recv, msg_send, msg_recv,
    row_send, row_recv, col_send, col_recv, known,
):
    tile = obj.shape[2]
    mid_rows = tile - 2 * HALO
    wide = 2 * HALO
    row, col = lax.axis_index("row"), lax.axis_index("col")
    odd = lax.rem(col, 2)
    step = 1 - 2 * odd
    near = 1 - odd
    far = odd
    partner, other = col + step, col - step
    ahead, behind = col + 2 * step, col - 2 * step
    has_other = (other >= 0) & (other < cols)
    has_ahead = (ahead >= 0) & (ahead < cols)
    has_behind = (behind >= 0) & (behind < cols)
    has_north, has_south = row > 0, row < rows - 1
    always = row >= 0

    def flip(value, bit):
        return value + bit * (1 - 2 * lax.rem(value // bit, 2))

    row_bits = [1 << k for k in range(rows.bit_length() - 1)]
    base, length, row_down, row_keep = 0, rows, [], []
    for k, bit in enumerate(row_bits):
        length = length // 2
        upper = lax.rem(row // bit, 2)
        keep, give = base + upper * length, base + (1 - upper) * length
        landing = buf1.at[pl.ds(rows - 2 * length, length)]
        row_down.append(pltpu.make_async_remote_copy(
            src_ref=prev.at[pl.ds(give, length)], dst_ref=landing, send_sem=row_send.at[0, k],
            recv_sem=row_recv.at[0, k], device_id=(flip(row, bit), col), device_id_type=MESH))
        row_keep.append((keep, length, landing))
        base = keep
    slot = base
    row_up = {}
    for k, bit in enumerate(reversed(row_bits)):
        for held in range(1 << k):
            where = slot
            for t in range(k):
                where = flip(where, 1 << t) if held >> t & 1 else where
            here, index = out_probe.at[where], held | 1 << k
            row_up[index] = pltpu.make_async_remote_copy(
                src_ref=here, dst_ref=here, send_sem=row_send.at[1, index - 1],
                recv_sem=row_recv.at[1, index - 1], device_id=(flip(row, bit), col), device_id_type=MESH)

    def spread_rows(held):
        if held:
            row_up[held].wait_recv()
        for k in range(held.bit_length(), len(row_bits)):
            row_up[held | 1 << k].start()

    fetches = [
        pltpu.make_async_copy(src, dst, local_sem.at[k])
        for k, (src, dst) in enumerate(
            ((obj_hbm.at[0], obj.at[0]), (obj_hbm.at[1], obj.at[1]), (prev_hbm, prev),
             (probe_hbm, probe), (probe_k_hbm.at[slot, col], probe_piece),
             (table_hbm, table), (amp_hbm, amp))
        )
    ]
    for fetch in fetches:
        fetch.start()

    barrier = pltpu.get_barrier_semaphore()

    def greet(sem, r, c):
        pl.semaphore_signal(sem, inc=1, device_id=(r, c), device_id_type=MESH)

    bits = [1 << k for k in range(cols.bit_length() - 1)]
    expected = 0
    for t in range(1, rows):
        greet(barrier, lax.rem(row + t, rows), col)
        expected = expected + 1
    for ok, c in ((always, partner), (has_other, other), (has_ahead, ahead), (has_behind, behind)):
        @pl.when(ok)
        def _():
            greet(barrier, row, c)
        expected = expected + ok.astype(jnp.int32)
    for bit in bits[2:]:
        greet(barrier, row, flip(col, bit))
        expected = expected + 1

    top, left = offs[0], offs[1]
    my_off[0] = jnp.zeros((8, wide), jnp.int32) + top
    my_off[1] = jnp.zeros((8, wide), jnp.int32) + left

    lane = lax.broadcasted_iota(jnp.int32, (1, wide), 1)
    first = lane < HALO
    lane64 = jnp.where(first, lane, lane - HALO)
    line = lax.broadcasted_iota(jnp.int32, (wide, 1), 0)

    def swap(value):
        return pltpu.roll(value, HALO, 1)

    def turned(index, corner):
        return (index < corner - HALO) | (index >= corner + HALO)

    def pack(ref, slot):
        re, im = ref
        if slot == 0:
            return jnp.where(first, re[:, :wide], swap(im[:, :wide]))
        return jnp.where(first, swap(re[:, tile - wide :]), im[:, tile - wide :])

    def ends(value):
        return cat([value[:HALO], value[tile - HALO :]], 0)

    for s in range(2):
        fetches[s].wait()
        for side in range(2):
            value = pack((obj[s, 0], obj[s, 1]), side)
            strip_mid[side, s] = value[HALO : tile - HALO]
            strip_edge[side, s] = ends(value)
    fetches[3].wait()
    turn_rows = lax.rem(top + tile - HALO, tile)
    turn_cols = lax.rem(left + tile - HALO, tile)
    for k in range(2):
        probe[k] = pltpu.roll(pltpu.roll(probe[k], turn_rows, 0), turn_cols, 1)

    fetches[6].wait()
    count_half = tile // 2

    def order(axis):
        target = lax.broadcasted_iota(jnp.int32, (tile, tile), axis)
        source = lax.broadcasted_iota(jnp.int32, (tile, tile), 1 - axis)
        target = jnp.where(target < count_half, 2 * target, 2 * (target - count_half) + 1)
        return (source == target).astype(jnp.float32).astype(jnp.bfloat16)

    ordered = dot(cat([order(0), order(0)], 1), cat(split(amp[...]), 0))
    amp[...] = dot(cat(split(ordered), 1), cat([order(1), order(1)], 0))

    @pl.when(jnp.logical_not(has_other))
    def _():
        off[far] = jnp.full((2, 8, wide), HALO, jnp.int32)

    for s in range(2):
        @pl.when(jnp.logical_not(has_south))
        def _():
            ns_in[s, :, :HALO, :] = jnp.zeros((2, HALO, tile), jnp.float32)
            ns_back[s, :, HALO:, :] = jnp.zeros((2, HALO, tile), jnp.float32)

        @pl.when(jnp.logical_not(has_north))
        def _():
            ns_in[s, :, HALO:, :] = jnp.zeros((2, HALO, tile), jnp.float32)
            ns_back[s, :, :HALO, :] = jnp.zeros((2, HALO, tile), jnp.float32)

        @pl.when(jnp.logical_not(has_ahead))
        def _():
            far_mid[s] = jnp.zeros((mid_rows, wide), jnp.float32)
            far_edge[s] = jnp.zeros((wide, wide), jnp.float32)

        @pl.when(jnp.logical_not(has_behind))
        def _():
            gs_mid[far, s] = jnp.zeros((mid_rows, wide), jnp.float32)
            gs_edge[far, s] = jnp.zeros((wide, wide), jnp.float32)

    class Link:
        def __init__(self, src, dst, send_sem, recv_sem, device, ok, inbound):
            self.copy = pltpu.make_async_remote_copy(
                src_ref=src, dst_ref=dst, send_sem=send_sem, recv_sem=recv_sem,
                device_id=device, device_id_type=MESH)
            self.ok, self.inbound = ok, inbound

        def start(self):
            @pl.when(self.ok)
            def _():
                self.copy.start()

        def arrive(self):
            @pl.when(self.inbound)
            def _():
                self.copy.wait_recv()

        def sent(self):
            @pl.when(self.ok)
            def _():
                self.copy.wait_send()

    up, down = slice(0, HALO), slice(HALO, wide)
    off_near = Link(my_off, off.at[1 - near], off_send.at[0], off_recv.at[0], (row, partner), always, always)
    off_far = Link(my_off, off.at[1 - far], off_send.at[1], off_recv.at[1], (row, other), has_other, has_other)

    def ns_links(phase, s):
        if phase == 0:
            src_up, src_down, dst = obj.at[s, :, up, :], obj.at[s, :, tile - HALO :, :], ns_in
            to_up, to_down = (row - 1, has_north, has_south), (row + 1, has_south, has_north)
        else:
            src_up, src_down, dst = ns_out.at[s, :, up, :], ns_out.at[s, :, down, :], ns_back
            to_up, to_down = (row + 1, has_south, has_north), (row - 1, has_north, has_south)
        return [
            Link(src, dst.at[s, :, span, :], ns_send.at[phase, s, k], ns_recv.at[phase, s, k], (to[0], col), to[1], to[2])
            for k, (src, span, to) in enumerate(((src_up, up, to_up), (src_down, down, to_down)))
        ]

    ns = [[ns_links(phase, s) for s in range(2)] for phase in range(2)]
    MID, EDGE = 0, 1
    far_link = [
        [
            Link(strip_mid.at[far, s], far_mid.at[s], far_send.at[0, s, 0], far_recv.at[0, s, 0], (row, behind), has_behind, has_ahead),
            Link(fold_far.at[s], far_edge.at[s], far_send.at[0, s, 1], far_recv.at[0, s, 1], (row, behind), has_behind, has_ahead),
        ]
        for s in range(2)
    ]
    msg_link = [
        [
            Link(msg_mid.at[s], got_mid.at[s], msg_send.at[0, s, 0], msg_recv.at[0, s, 0], (row, partner), always, always),
            Link(msg_edge.at[s], got_edge.at[s], msg_send.at[0, s, 1], msg_recv.at[0, s, 1], (row, partner), always, always),
        ]
        for s in range(2)
    ]
    gmsg_link = [
        [
            Link(gmsg_mid.at[s], gs_mid.at[1 - near, s], msg_send.at[1, s, 0], msg_recv.at[1, s, 0], (row, partner), always, always),
            Link(gmsg_edge.at[s], gs_edge.at[1 - near, s], msg_send.at[1, s, 1], msg_recv.at[1, s, 1], (row, partner), always, always),
        ]
        for s in range(2)
    ]
    pass_link = [
        [
            Link(gs_mid.at[near, s], gs_mid.at[far, s], far_send.at[1, s, 0], far_recv.at[1, s, 0], (row, ahead), has_ahead, has_behind),
            Link(gs_edge.at[near, s], gs_edge.at[far, s], far_send.at[1, s, 1], far_recv.at[1, s, 1], (row, ahead), has_ahead, has_behind),
        ]
        for s in range(2)
    ]

    def add_rows(k):
        keep, count_rows, landing = row_keep[k]
        row_down[k].wait_recv()
        prev[pl.ds(keep, count_rows)] += landing[...]

    def col_copies(stage):
        made = []
        for t in range(1, cols):
            peer = lax.rem(col + t, cols)
            if stage == 0:
                src, dst = prev.at[slot, peer], buf2.at[t - 1]
            else:
                src, dst = out_probe.at[slot, col], out_probe.at[slot, col]
            made.append(pltpu.make_async_remote_copy(
                src_ref=src, dst_ref=dst, send_sem=col_send.at[stage, t - 1],
                recv_sem=col_recv.at[stage, t - 1], device_id=(row, peer), device_id_type=MESH))
        return made

    fetches[2].wait()
    pl.semaphore_wait(barrier, expected)

    off_near.start()
    off_far.start()
    row_down[0].start()
    for s in range(2):
        for link in ns[0][s]:
            link.start()
        far_link[s][MID].start()
    for bit in bits:
        greet(known.at[0], row, flip(col, bit))

    off_near.arrive()
    off_far.arrive()
    near_off, far_off = off[near], off[far]
    near_top, near_left = near_off[0, :1], near_off[1, :1]
    far_top = far_off[0, :1]
    take_own = jnp.where(near == 0, near_left - HALO, HALO - near_left) > 0

    def fold(s):
        for link in ns[0][s]:
            link.arrive()
        packs = [pack((ns_in[s, 0], ns_in[s, 1]), slot) for slot in range(2)]
        far_pack = jnp.where(far == 0, packs[0], packs[1])
        near_pack = jnp.where(near == 0, packs[0], packs[1])
        fold_far[s] = jnp.where(turned(line, far_top), far_pack, strip_edge[far, s])
        far_link[s][EDGE].start()
        msg_edge[s] = jnp.where(turned(line, near_top), near_pack, strip_edge[near, s])

    def forward_mid(s):
        far_link[s][MID].arrive()
        msg_mid[s] = jnp.where(take_own, strip_mid[near, s], far_mid[s])
        msg_link[s][MID].start()

    def forward_edge(s):
        far_link[s][EDGE].arrive()
        msg_edge[s] = jnp.where(take_own, msg_edge[s], far_edge[s])
        msg_link[s][EDGE].start()

    add_rows(0)
    for k in range(1, len(row_bits)):
        row_down[k].start()
        if k + 1 < len(row_bits):
            add_rows(k)
    fold(0)
    forward_mid(0)
    fold(1)
    forward_mid(1)
    forward_edge(0)
    forward_edge(1)

    for wait_round, bit in enumerate(bits[1:]):
        pl.semaphore_wait(known.at[wait_round], len(bits))
        if wait_round + 1 < len(bits) - 1:
            for again in bits:
                greet(known.at[wait_round + 1], row, flip(col, again))

    def assemble(s):
        from_east, from_west = lane < left - HALO, lane >= left + HALO

        def columns(base, strip):
            turned_strip = swap(strip)
            for k in range(2):
                re_like, im_like = (strip, turned_strip) if k == 0 else (turned_strip, strip)
                head = jnp.where(from_east, re_like, base[k][:, :wide])
                tail = jnp.where(from_west, im_like, base[k][:, tile - wide :])
                yield cat([head, base[k][:, wide : tile - wide], tail], 1) if tile > 2 * wide else cat([head, tail], 1)

        msg_link[s][MID].arrive()
        for k, value in enumerate(columns([obj[s, p, HALO : tile - HALO, :] for p in range(2)], got_mid[s])):
            z[s, k, HALO : tile - HALO, :] = value
        msg_link[s][EDGE].arrive()
        base = [jnp.where(turned(line, top), ns_in[s, p], ends(obj[s, p])) for p in range(2)]
        for k, value in enumerate(columns(base, got_edge[s])):
            z[s, k, :HALO, :] = value[:HALO]
            z[s, k, tile - HALO :, :] = value[HALO:]

    def back(s, gre, gim):
        east = jnp.where(lane64 < left - HALO, pack((gre, gim), 0), 0.0)
        west = jnp.where(lane64 >= left, pack((gre, gim), 1), 0.0)
        value = jnp.where(left > HALO, east, west)
        gmsg_edge[s] = ends(value)
        gmsg_link[s][EDGE].start()
        gmsg_mid[s] = value[HALO : tile - HALO]
        gmsg_link[s][MID].start()
        away = turned(line, top)
        lanes = lax.broadcasted_iota(jnp.int32, (1, tile), 1)
        stay = jnp.logical_not((lanes < left - HALO) | (lanes >= left + tile - HALO))
        for k, grad in enumerate((gre, gim)):
            grad = jnp.where(stay, grad, 0.0)
            acc_mid[s, k] = grad[HALO : tile - HALO]
            edge = ends(grad)
            acc_edge[s, k] = jnp.where(away, 0.0, edge)
            ns_out[s, k] = jnp.where(away, edge, 0.0)

    if len(row_bits) > 1:
        add_rows(len(row_bits) - 1)
    rs_cols = col_copies(0)
    for copy in rs_cols:
        copy.start()

    fetches[5].wait()
    assemble(0)
    ar, ai = z[0, 0], z[0, 1]
    pr, pi = probe[0], probe[1]
    vr, vi = sandwich(pr * ar - pi * ai, pr * ai + pi * ar, table, 1, False)

    assemble(1)
    br, bi = z[1, 0], z[1, 1]
    wr, wi = sandwich(vr * br - vi * bi, vr * bi + vi * br, table, 0, False)
    live = jnp.where(count[0] > 0, 2.0, 0.0)
    scale = live - (live * amp[...]) * lax.rsqrt(wr * wr + wi * wi + 1.0)
    xr, xi = sandwich(scale * wr, scale * wi, table, 0, True)
    back(1, xr * vr + xi * vi, xi * vr - xr * vi)

    for copy in rs_cols:
        copy.wait_recv()
    fetches[4].wait()
    total = prev[slot, col]
    for t in range(1, cols):
        total = total + buf2[t - 1]
    rate = PROBE_RATE / math.sqrt(rows * cols)
    out_probe[slot, col] = probe_piece[...] - rate * total
    ag_cols = col_copies(1)
    for copy in ag_cols:
        copy.start()


    ur, ui = sandwich(xr * br + xi * bi, xi * br - xr * bi, table, 1, True)
    back(0, ur * pr + ui * pi, ui * pr - ur * pi)

    for s in (1,):
        for piece in (EDGE, MID):
            gmsg_link[s][piece].arrive()
            pass_link[s][piece].start()

    for copy in ag_cols:
        copy.wait_recv()
    spread_rows(0)

    for s in (0,):
        for piece in (EDGE, MID):
            gmsg_link[s][piece].arrive()
            pass_link[s][piece].start()

    home_rows = lax.rem(tile + HALO - top, tile)
    home_cols = lax.rem(tile + HALO - left, tile)
    out_part[0] = pltpu.roll(pltpu.roll(ur * ar + ui * ai, home_rows, 0), home_cols, 1)
    out_part[1] = pltpu.roll(pltpu.roll(ui * ar - ur * ai, home_rows, 0), home_cols, 1)

    head_off, tail_off = off[0], off[1]
    accept = (head_off[1, :1] > HALO, tail_off[1, :1] < HALO)
    corner = (head_off[0, :1], tail_off[0, :1])
    span = (slice(0, wide), slice(tile - wide, tile))

    def parts_of(slot, strip):
        if slot == 0:
            return jnp.where(first, strip, 0.0), jnp.where(first, swap(strip), 0.0)
        return jnp.where(first, 0.0, swap(strip)), jnp.where(first, 0.0, strip)

    def collect_edge(s):
        pass_link[s][EDGE].arrive()
        for slot in range(2):
            strip = jnp.where(accept[slot], gs_edge[slot, s], 0.0)
            moves = turned(line, corner[slot])
            for dst, kept in ((ns_out, jnp.where(moves, strip, 0.0)), (acc_edge, jnp.where(moves, 0.0, strip))):
                for k, value in enumerate(parts_of(slot, kept)):
                    dst[s, k, :, span[slot]] += value
        for link in ns[1][s]:
            link.start()

    def collect_mid(s):
        pass_link[s][MID].arrive()
        for slot in range(2):
            strip = jnp.where(accept[slot], gs_mid[slot, s], 0.0)
            for k, value in enumerate(parts_of(slot, strip)):
                acc_mid[s, k, :, span[slot]] += value
        for k in range(2):
            out_obj[s, k, HALO : tile - HALO, :] = obj[s, k, HALO : tile - HALO, :] - OBJ_RATE * acc_mid[s, k]

    def finish_edge(s):
        for link in ns[1][s]:
            link.arrive()
        for k in range(2):
            value = ends(obj[s, k]) - OBJ_RATE * (acc_edge[s, k] + ns_back[s, k])
            out_obj[s, k, :HALO, :] = value[:HALO]
            out_obj[s, k, tile - HALO :, :] = value[HALO:]

    collect_edge(1)
    collect_edge(0)
    for held in range(1, rows):
        spread_rows(held)
    collect_mid(1)
    collect_mid(0)
    finish_edge(1)
    finish_edge(0)

    off_near.sent()
    off_far.sent()
    for s in range(2):
        for phase in range(2):
            for link in ns[phase][s]:
                link.sent()
        for piece in range(2):
            for group in (far_link, msg_link, gmsg_link, pass_link):
                group[s][piece].sent()
    for copy in row_down + rs_cols + ag_cols + list(row_up.values()):
        copy.wait_send()


def store(obj, probe, part, out_obj, out_probe, out_part, sem):
    copies = [
        pltpu.make_async_copy(src, dst, sem.at[k])
        for k, (src, dst) in enumerate(((obj, out_obj), (probe, out_probe), (part, out_part)))
    ]
    for copy in copies:
        copy.start()
    for copy in copies:
        copy.wait()


def shards(rows, cols, objects, probe, prev_partial, offsets, counts, amplitudes):
    tile = objects.shape[2]
    win = probe.shape[-1]
    assert tile == win and cols % 2 == 0
    piece = (2 * win) // (rows * cols)
    split_shape = (rows, cols, piece, win)
    table = jnp.asarray(operator_table(win))
    f32 = jnp.float32
    smem = pl.BlockSpec(memory_space=pltpu.SMEM)
    anyspace = pl.BlockSpec(memory_space=pl.ANY)
    vmem = pl.BlockSpec(memory_space=pltpu.VMEM)
    V = lambda *shape: pltpu.VMEM(shape, f32)
    mid, wide = tile - 2 * HALO, 2 * HALO
    dma = pltpu.SemaphoreType.DMA
    scratch = [
        V(2, 2, tile, tile), V(*split_shape), V(2, win, win), V(piece, win), V(win, win),
        pltpu.VMEM(table.shape, jnp.bfloat16),
        pltpu.VMEM((2, 8, wide), jnp.int32), pltpu.VMEM((2, 2, 8, wide), jnp.int32),
        V(2, 2, wide, tile), V(2, 2, mid, wide), V(2, 2, wide, wide), V(2, wide, wide),
        V(2, mid, wide), V(2, wide, wide), V(2, mid, wide), V(2, wide, wide), V(2, mid, wide), V(2, wide, wide),
        V(2, 2, tile, tile),
        V(2, mid, wide), V(2, wide, wide), V(2, 2, mid, wide), V(2, 2, wide, wide),
        V(2, 2, mid, tile), V(2, 2, wide, tile), V(2, 2, wide, tile), V(2, 2, wide, tile),
        V(max(rows - 1, 1), cols, piece, win), V(max(cols - 1, 1), piece, win),
        dma((7,)), dma((2,)), dma((2,)), dma((2, 2, 2)), dma((2, 2, 2)),
        dma((2, 2, 2)), dma((2, 2, 2)), dma((2, 2, 2)), dma((2, 2, 2)),
        dma((2, max(rows - 1, 1))), dma((2, max(rows - 1, 1))),
        dma((2, max(cols - 1, 1))), dma((2, max(cols - 1, 1))),
        pltpu.SemaphoreType.REGULAR((max(cols.bit_length() - 2, 1),)),
    ]
    results = pl.pallas_call(
        functools.partial(kernel, rows, cols),
        out_shape=(
            pltpu.VMEM(objects.shape, f32), pltpu.VMEM(split_shape, f32), pltpu.VMEM(probe.shape, f32),
        ),
        in_specs=[smem, smem] + [anyspace] * 6,
        out_specs=(vmem, vmem, vmem),
        scratch_shapes=scratch,
        compiler_params=pltpu.CompilerParams(
            collective_id=0, has_side_effects=True, vmem_limit_bytes=56 * 2**20
        ),
    )(
        offsets.reshape(2), counts.reshape(1), objects, prev_partial.reshape(split_shape),
        probe, probe.reshape(split_shape), amplitudes.reshape(win, win), table,
    )
    new_obj, new_probe, part = pl.pallas_call(
        store,
        out_shape=tuple(jax.ShapeDtypeStruct(v.shape, f32) for v in results),
        in_specs=[vmem] * 3,
        out_specs=(pl.BlockSpec(memory_space=pltpu.HBM),) * 3,
        scratch_shapes=[dma((3,))],
    )(*[pltpu.with_memory_space_constraint(v, pltpu.VMEM) for v in results])
    return new_obj, new_probe.reshape(probe.shape), part[None, None]


def solution(mesh):
    in_specs = (
        P(None, None, "row", "col"),
        P(),
        P("row", "col", None, None, None),
        P("row", "col", None, None),
        P("row", "col"),
        P("row", "col", None, None, None),
    )
    out_specs = (P(None, None, "row", "col"), P(), P("row", "col", None, None, None))
    body = functools.partial(shards, mesh.shape["row"], mesh.shape["col"])
    return jax.shard_map(body, mesh=mesh, in_specs=in_specs, out_specs=out_specs, check_vma=False)
```

```python
import functools
import math

import jax
import jax.numpy as jnp
import numpy as np
from jax import lax
from jax.experimental import pallas as pl
from jax.experimental.pallas import tpu as pltpu
from jax.sharding import PartitionSpec as P

HALO = 64
OBJ_RATE = 0.1
PROBE_RATE = 0.3
MESH = pl.DeviceIdType.MESH


def split(value):
    high = value.astype(jnp.bfloat16)
    low = (value - high.astype(jnp.float32)).astype(jnp.bfloat16)
    return high, low


def operator_table(n):
    half = n // 2
    index = np.arange(n)
    dft = np.exp(-2j * np.pi * (np.outer(index, index) % n) / n) / np.sqrt(n)
    freq = np.where(index < half, index, index - n).astype(np.float64)
    phase = np.exp(1j * np.pi * freq * freq / (4.0 * n))
    prop = np.conj(dft) @ (phase[:, None] * dft)
    near, far = prop[:half, :half], prop[:half, half:]
    tables = []
    for mat in (dft[0::2, :half], dft[1::2, :half], (near + far) / 2, (near - far) / 2):
        right = np.block([[mat.real.T, mat.imag.T], [-mat.imag.T, mat.real.T]]).astype(np.float32)
        for part in (right, right.T):
            high = part.astype(jnp.bfloat16)
            tables += [high, (part - high.astype(np.float32)).astype(jnp.bfloat16)]
    return np.stack(tables).reshape(2, 2, 2, 2, n, n)


def dot(left, right):
    return jnp.dot(left, right, preferred_element_type=jnp.float32)


def cat(parts, axis):
    return jnp.concatenate(parts, axis=axis)


def times(data, table, which, side, flip):
    kind = int(flip if side else not flip)
    out = []
    for k in range(2):
        high, low = table[which, k, kind, 0], table[which, k, kind, 1]
        dh, dl = split(data[k])
        if side:
            out.append(dot(cat([dh, dl, dh], 1), cat([high, high, low], 0)))
        else:
            out.append(dot(cat([high, high, low], 1), cat([dh, dl, dh], 0)))
    return out


def halves(value, axis):
    half = value.shape[axis] // 2
    return (value[:half], value[half:]) if axis == 0 else (value[:, :half], value[:, half:])


def transform(re, im, table, which, axis, merge, divide, flip):
    if divide:
        parts = [halves(v, axis) for v in (re, im)]
        data = [cat([a + b for a, b in parts], axis), cat([a - b for a, b in parts], axis)]
    else:
        parts = [halves(v, axis) for v in (re, im)]
        data = [cat([p[0] for p in parts], axis), cat([p[1] for p in parts], axis)]
    even, odd = [halves(v, axis) for v in times(data, table, which, axis, flip)]
    if merge:
        return [cat([a + b, a - b], axis) for a, b in zip(even, odd)]
    return [cat([a, b], axis) for a, b in zip(even, odd)]


def sandwich(xr, xi, table, which, conj):
    divide = which == 1 or not conj
    merge = which == 1 or conj
    tr, ti = transform(xr, xi, table, which, 1, merge, divide, conj)
    return transform(tr, ti, table, which, 0, merge, divide, conj)


def kernel(
    rows, cols, offs, count, obj_hbm, prev_hbm, probe_hbm, probe_k_hbm, amp_hbm, table_hbm,
    out_obj, out_probe, out_part,
    obj, prev, probe, probe_piece, amp, table,
    my_off, off,
    strip_mid, strip_edge, inner_edge, ns_pack, ns_inner, fold_far, far_mid, far_edge, msg_mid, msg_edge, got_mid, got_edge, z,
    gmsg_mid, gmsg_edge, gs_mid, gs_edge, pack_out, inner_out, pack_mid, pack_edge, in_mid, in_edge,
    buf1, buf2,
    local_sem, off_send, off_recv, ns_send, ns_recv, far_send, far_recv, msg_send, msg_recv,
    row_send, row_recv, col_send, col_recv, known,
):
    tile = obj.shape[2]
    mid_rows = tile - 2 * HALO
    wide = 2 * HALO
    row, col = lax.axis_index("row"), lax.axis_index("col")
    odd = lax.rem(col, 2)
    step = 1 - 2 * odd
    near = 1 - odd
    far = odd
    partner, other = col + step, col - step
    ahead, behind = col + 2 * step, col - 2 * step
    has_other = (other >= 0) & (other < cols)
    has_ahead = (ahead >= 0) & (ahead < cols)
    has_behind = (behind >= 0) & (behind < cols)
    has_north, has_south = row > 0, row < rows - 1
    always = row >= 0

    def flip(value, bit):
        return value + bit * (1 - 2 * lax.rem(value // bit, 2))

    row_bits = [1 << k for k in range(rows.bit_length() - 1)]
    base, length, row_down, row_keep = 0, rows, [], []
    for k, bit in enumerate(row_bits):
        length = length // 2
        upper = lax.rem(row // bit, 2)
        keep, give = base + upper * length, base + (1 - upper) * length
        landing = buf1.at[pl.ds(rows - 2 * length, length)]
        row_down.append(pltpu.make_async_remote_copy(
            src_ref=prev.at[pl.ds(give, length)], dst_ref=landing, send_sem=row_send.at[0, k],
            recv_sem=row_recv.at[0, k], device_id=(flip(row, bit), col), device_id_type=MESH))
        row_keep.append((keep, length, landing))
        base = keep
    slot = base
    row_up = {}
    for k, bit in enumerate(reversed(row_bits)):
        for held in range(1 << k):
            where = slot
            for t in range(k):
                where = flip(where, 1 << t) if held >> t & 1 else where
            here, index = out_probe.at[where], held | 1 << k
            row_up[index] = pltpu.make_async_remote_copy(
                src_ref=here, dst_ref=here, send_sem=row_send.at[1, index - 1],
                recv_sem=row_recv.at[1, index - 1], device_id=(flip(row, bit), col), device_id_type=MESH)

    def spread_rows(held):
        if held:
            row_up[held].wait_recv()
        for k in range(held.bit_length(), len(row_bits)):
            row_up[held | 1 << k].start()

    fetches = [
        pltpu.make_async_copy(src, dst, local_sem.at[k])
        for k, (src, dst) in enumerate(
            ((obj_hbm.at[0], obj.at[0]), (obj_hbm.at[1], obj.at[1]), (prev_hbm, prev),
             (probe_hbm, probe), (probe_k_hbm.at[slot, col], probe_piece),
             (table_hbm, table), (amp_hbm, amp))
        )
    ]
    for fetch in fetches:
        fetch.start()

    barrier = pltpu.get_barrier_semaphore()

    def greet(sem, r, c):
        pl.semaphore_signal(sem, inc=1, device_id=(r, c), device_id_type=MESH)

    bits = [1 << k for k in range(cols.bit_length() - 1)]
    expected = 0
    for t in range(1, rows):
        greet(barrier, lax.rem(row + t, rows), col)
        expected = expected + 1
    for ok, c in ((always, partner), (has_other, other), (has_ahead, ahead), (has_behind, behind)):
        @pl.when(ok)
        def _():
            greet(barrier, row, c)
        expected = expected + ok.astype(jnp.int32)
    for bit in bits[2:]:
        greet(barrier, row, flip(col, bit))
        expected = expected + 1

    top, left = offs[0], offs[1]
    my_off[0] = jnp.zeros((8, wide), jnp.int32) + top
    my_off[1] = jnp.zeros((8, wide), jnp.int32) + left

    lane = lax.broadcasted_iota(jnp.int32, (1, wide), 1)
    first = lane < HALO
    lane64 = jnp.where(first, lane, lane - HALO)
    line = lax.broadcasted_iota(jnp.int32, (wide, 1), 0)

    def swap(value):
        return pltpu.roll(value, HALO, 1)

    def turned(index, corner):
        return (index < corner - HALO) | (index >= corner + HALO)

    def pack(ref, slot):
        re, im = ref
        if slot == 0:
            return jnp.where(first, re[:, :wide], swap(im[:, :wide]))
        return jnp.where(first, swap(re[:, tile - wide :]), im[:, tile - wide :])

    def inner_of(value):
        return jnp.where(first, value[:, wide:], value[:, :wide])

    def unpack(head, tail, inner):
        re = cat([jnp.where(first, head, inner[0]), jnp.where(first, inner[0], swap(tail))], 1)
        im = cat([jnp.where(first, swap(head), inner[1]), jnp.where(first, inner[1], tail)], 1)
        return re, im

    def ends(value):
        return cat([value[:HALO], value[tile - HALO :]], 0)

    for s in range(2):
        fetches[s].wait()
        for side in range(2):
            value = pack((obj[s, 0], obj[s, 1]), side)
            strip_mid[side, s] = value[HALO : tile - HALO]
            strip_edge[side, s] = ends(value)
        for k in range(2):
            inner_edge[s, k] = inner_of(ends(obj[s, k]))
    fetches[3].wait()
    turn_rows = lax.rem(top + tile - HALO, tile)
    turn_cols = lax.rem(left + tile - HALO, tile)
    for k in range(2):
        probe[k] = pltpu.roll(pltpu.roll(probe[k], turn_rows, 0), turn_cols, 1)

    fetches[6].wait()
    count_half = tile // 2

    def order(axis):
        target = lax.broadcasted_iota(jnp.int32, (tile, tile), axis)
        source = lax.broadcasted_iota(jnp.int32, (tile, tile), 1 - axis)
        target = jnp.where(target < count_half, 2 * target, 2 * (target - count_half) + 1)
        return (source == target).astype(jnp.float32).astype(jnp.bfloat16)

    ordered = dot(cat([order(0), order(0)], 1), cat(split(amp[...]), 0))
    amp[...] = dot(cat(split(ordered), 1), cat([order(1), order(1)], 0))

    @pl.when(jnp.logical_not(has_other))
    def _():
        off[far] = jnp.full((2, 8, wide), HALO, jnp.int32)

    for s in range(2):
        for phase, spans in ((0, ((has_south, slice(0, HALO)), (has_north, slice(HALO, wide)))),
                             (1, ((has_north, slice(0, HALO)), (has_south, slice(HALO, wide))))):
            for ok, span in spans:
                @pl.when(jnp.logical_not(ok))
                def _():
                    ns_pack[phase, s, :, span, :] = jnp.zeros((2, HALO, wide), jnp.float32)
                    ns_inner[phase, s, :, span, :] = jnp.zeros((2, HALO, wide), jnp.float32)

        @pl.when(jnp.logical_not(has_ahead))
        def _():
            far_mid[s] = jnp.zeros((mid_rows, wide), jnp.float32)
            far_edge[s] = jnp.zeros((wide, wide), jnp.float32)

        @pl.when(jnp.logical_not(has_behind))
        def _():
            gs_mid[far, s] = jnp.zeros((mid_rows, wide), jnp.float32)
            gs_edge[far, s] = jnp.zeros((wide, wide), jnp.float32)

    class Link:
        def __init__(self, src, dst, send_sem, recv_sem, device, ok, inbound):
            self.copy = pltpu.make_async_remote_copy(
                src_ref=src, dst_ref=dst, send_sem=send_sem, recv_sem=recv_sem,
                device_id=device, device_id_type=MESH)
            self.ok, self.inbound = ok, inbound

        def start(self):
            @pl.when(self.ok)
            def _():
                self.copy.start()

        def arrive(self):
            @pl.when(self.inbound)
            def _():
                self.copy.wait_recv()

        def sent(self):
            @pl.when(self.ok)
            def _():
                self.copy.wait_send()

    up, down = slice(0, HALO), slice(HALO, wide)
    off_near = Link(my_off, off.at[1 - near], off_send.at[0], off_recv.at[0], (row, partner), always, always)
    off_far = Link(my_off, off.at[1 - far], off_send.at[1], off_recv.at[1], (row, other), has_other, has_other)

    north, south = (row - 1, has_north, has_south), (row + 1, has_south, has_north)

    def ns_links(phase, s, kind):
        if kind == 0:
            src = strip_edge.at[:, s] if phase == 0 else pack_out.at[s]
            dst = ns_pack.at[phase, s]
        else:
            src = (inner_edge if phase == 0 else inner_out).at[s]
            dst = ns_inner.at[phase, s]
        made = []
        for k, (span, to) in enumerate(((up, south if phase else north), (down, north if phase else south))):
            sem = 2 * kind + k
            made.append(Link(src.at[:, span, :], dst.at[:, span, :], ns_send.at[phase, s, sem], ns_recv.at[phase, s, sem],
                             (to[0], col), to[1], to[2]))
        return made

    PACK, INNER = 0, 1
    ns = [[[ns_links(phase, s, kind) for kind in range(2)] for s in range(2)] for phase in range(2)]
    MID, EDGE = 0, 1
    far_link = [
        [
            Link(strip_mid.at[far, s], far_mid.at[s], far_send.at[0, s, 0], far_recv.at[0, s, 0], (row, behind), has_behind, has_ahead),
            Link(fold_far.at[s], far_edge.at[s], far_send.at[0, s, 1], far_recv.at[0, s, 1], (row, behind), has_behind, has_ahead),
        ]
        for s in range(2)
    ]
    msg_link = [
        [
            Link(msg_mid.at[s], got_mid.at[s], msg_send.at[0, s, 0], msg_recv.at[0, s, 0], (row, partner), always, always),
            Link(msg_edge.at[s], got_edge.at[s], msg_send.at[0, s, 1], msg_recv.at[0, s, 1], (row, partner), always, always),
        ]
        for s in range(2)
    ]
    gmsg_link = [
        [
            Link(gmsg_mid.at[s], gs_mid.at[1 - near, s], msg_send.at[1, s, 0], msg_recv.at[1, s, 0], (row, partner), always, always),
            Link(gmsg_edge.at[s], gs_edge.at[1 - near, s], msg_send.at[1, s, 1], msg_recv.at[1, s, 1], (row, partner), always, always),
        ]
        for s in range(2)
    ]
    pass_link = [
        [
            Link(gs_mid.at[near, s], gs_mid.at[far, s], far_send.at[1, s, 0], far_recv.at[1, s, 0], (row, ahead), has_ahead, has_behind),
            Link(gs_edge.at[near, s], gs_edge.at[far, s], far_send.at[1, s, 1], far_recv.at[1, s, 1], (row, ahead), has_ahead, has_behind),
        ]
        for s in range(2)
    ]

    def add_rows(k):
        keep, count_rows, landing = row_keep[k]
        row_down[k].wait_recv()
        prev[pl.ds(keep, count_rows)] += landing[...]

    def col_copies(stage):
        made = []
        for t in range(1, cols):
            peer = lax.rem(col + t, cols)
            if stage == 0:
                src, dst = prev.at[slot, peer], buf2.at[t - 1]
            else:
                src, dst = out_probe.at[slot, col], out_probe.at[slot, col]
            made.append(pltpu.make_async_remote_copy(
                src_ref=src, dst_ref=dst, send_sem=col_send.at[stage, t - 1],
                recv_sem=col_recv.at[stage, t - 1], device_id=(row, peer), device_id_type=MESH))
        return made

    fetches[2].wait()
    pl.semaphore_wait(barrier, expected)

    off_near.start()
    off_far.start()
    row_down[0].start()
    for s in range(2):
        for link in ns[0][s][PACK]:
            link.start()
        far_link[s][MID].start()
    for s in range(2):
        for link in ns[0][s][INNER]:
            link.start()
    for bit in bits:
        greet(known.at[0], row, flip(col, bit))

    off_near.arrive()
    off_far.arrive()
    near_off, far_off = off[near], off[far]
    near_top, near_left = near_off[0, :1], near_off[1, :1]
    far_top = far_off[0, :1]
    take_own = jnp.where(near == 0, near_left - HALO, HALO - near_left) > 0

    def fold(s):
        for link in ns[0][s][PACK]:
            link.arrive()
        fold_far[s] = jnp.where(turned(line, far_top), ns_pack[0, s, far], strip_edge[far, s])
        far_link[s][EDGE].start()
        msg_edge[s] = jnp.where(turned(line, near_top), ns_pack[0, s, near], strip_edge[near, s])

    def forward_mid(s):
        far_link[s][MID].arrive()
        msg_mid[s] = jnp.where(take_own, strip_mid[near, s], far_mid[s])
        msg_link[s][MID].start()

    def forward_edge(s):
        far_link[s][EDGE].arrive()
        msg_edge[s] = jnp.where(take_own, msg_edge[s], far_edge[s])
        msg_link[s][EDGE].start()

    add_rows(0)
    for k in range(1, len(row_bits)):
        row_down[k].start()
        if k + 1 < len(row_bits):
            add_rows(k)
    fold(0)
    forward_mid(0)
    fold(1)
    forward_mid(1)
    forward_edge(0)
    forward_edge(1)

    for wait_round, bit in enumerate(bits[1:]):
        pl.semaphore_wait(known.at[wait_round], len(bits))
        if wait_round + 1 < len(bits) - 1:
            for again in bits:
                greet(known.at[wait_round + 1], row, flip(col, again))

    def assemble(s):
        from_east, from_west = lane64 < left - HALO, lane64 >= left

        msg_link[s][MID].arrive()
        packs = [jnp.where(take, got_mid[s], strip_mid[side, s]) for side, take in enumerate((from_east, from_west))]
        inner = [inner_of(obj[s, k, HALO : tile - HALO, :]) for k in range(2)]
        for k, value in enumerate(unpack(*packs, inner)):
            z[s, k, HALO : tile - HALO, :] = value
        for link in ns[0][s][INNER]:
            link.arrive()
        away = turned(line, top)
        inner = [jnp.where(away, ns_inner[0, s, k], inner_edge[s, k]) for k in range(2)]
        packs = [jnp.where(away, ns_pack[0, s, side], strip_edge[side, s]) for side in range(2)]
        msg_link[s][EDGE].arrive()
        packs = [jnp.where(take, got_edge[s], packs[side]) for side, take in enumerate((from_east, from_west))]
        for k, value in enumerate(unpack(*packs, inner)):
            z[s, k, :HALO, :] = value[:HALO]
            z[s, k, tile - HALO :, :] = value[HALO:]

    def back(s, gre, gim):
        leaves = lane64 < left - HALO, lane64 >= left
        packs = [pack((gre, gim), side) for side in range(2)]
        out = [jnp.where(leave, value, 0.0) for leave, value in zip(leaves, packs)]
        value = jnp.where(left > HALO, out[0], out[1])
        gmsg_edge[s] = ends(value)
        gmsg_link[s][EDGE].start()
        gmsg_mid[s] = value[HALO : tile - HALO]
        if s == 0:
            gmsg_link[1][MID].start()
            gmsg_link[0][MID].start()
        away = turned(line, top)
        inner = [inner_of(grad) for grad in (gre, gim)]
        for k in range(2):
            edge = ends(inner[k])
            inner_out[s, k] = jnp.where(away, edge, 0.0)
            in_edge[s, k] = jnp.where(away, 0.0, edge)
        for link in ns[1][s][INNER]:
            link.start()
        for k in range(2):
            in_mid[s, k] = inner[k][HALO : tile - HALO]
            stay = jnp.where(leaves[k], 0.0, packs[k])
            pack_mid[s, k] = stay[HALO : tile - HALO]
            edge = ends(stay)
            pack_out[s, k] = jnp.where(away, edge, 0.0)
            pack_edge[s, k] = jnp.where(away, 0.0, edge)

    if len(row_bits) > 1:
        add_rows(len(row_bits) - 1)
    rs_cols = col_copies(0)
    for copy in rs_cols:
        copy.start()

    fetches[5].wait()
    assemble(0)
    ar, ai = z[0, 0], z[0, 1]
    pr, pi = probe[0], probe[1]
    vr, vi = sandwich(pr * ar - pi * ai, pr * ai + pi * ar, table, 1, False)

    assemble(1)
    br, bi = z[1, 0], z[1, 1]
    wr, wi = sandwich(vr * br - vi * bi, vr * bi + vi * br, table, 0, False)
    live = jnp.where(count[0] > 0, 2.0, 0.0)
    scale = live - (live * amp[...]) * lax.rsqrt(wr * wr + wi * wi + 1.0)
    xr, xi = sandwich(scale * wr, scale * wi, table, 0, True)
    back(1, xr * vr + xi * vi, xi * vr - xr * vi)

    for copy in rs_cols:
        copy.wait_recv()
    fetches[4].wait()
    total = prev[slot, col]
    for t in range(1, cols):
        total = total + buf2[t - 1]
    rate = PROBE_RATE / math.sqrt(rows * cols)
    out_probe[slot, col] = probe_piece[...] - rate * total
    ag_cols = col_copies(1)
    for copy in ag_cols:
        copy.start()


    ur, ui = sandwich(xr * br + xi * bi, xi * br - xr * bi, table, 1, True)
    back(0, ur * pr + ui * pi, ui * pr - ur * pi)

    def relay(s, piece):
        gmsg_link[s][piece].arrive()
        pass_link[s][piece].start()

    relay(1, EDGE)
    for copy in ag_cols:
        copy.wait_recv()
    spread_rows(0)
    relay(0, EDGE)
    home_rows = lax.rem(tile + HALO - top, tile)
    home_cols = lax.rem(tile + HALO - left, tile)
    out_part[0] = pltpu.roll(pltpu.roll(ur * ar + ui * ai, home_rows, 0), home_cols, 1)
    out_part[1] = pltpu.roll(pltpu.roll(ui * ar - ur * ai, home_rows, 0), home_cols, 1)

    head_off, tail_off = off[0], off[1]
    accept = (head_off[1, :1] > HALO, tail_off[1, :1] < HALO)
    corner = (head_off[0, :1], tail_off[0, :1])

    def collect_edge(s):
        pass_link[s][EDGE].arrive()
        for side in range(2):
            strip = jnp.where(accept[side], gs_edge[side, s], 0.0)
            moves = turned(line, corner[side])
            pack_out[s, side] += jnp.where(moves, strip, 0.0)
            pack_edge[s, side] += jnp.where(moves, 0.0, strip)
        for link in ns[1][s][PACK]:
            link.start()

    def collect_mid(s):
        pass_link[s][MID].arrive()
        packs = [
            strip_mid[side, s] - OBJ_RATE * (pack_mid[s, side] + jnp.where(accept[side], gs_mid[side, s], 0.0))
            for side in range(2)
        ]
        inner = [inner_of(obj[s, k, HALO : tile - HALO, :]) - OBJ_RATE * in_mid[s, k] for k in range(2)]
        for k, value in enumerate(unpack(*packs, inner)):
            out_obj[s, k, HALO : tile - HALO, :] = value

    def finish_edge(s):
        for kind in (INNER, PACK):
            for link in ns[1][s][kind]:
                link.arrive()
        packs = [strip_edge[side, s] - OBJ_RATE * (pack_edge[s, side] + ns_pack[1, s, side]) for side in range(2)]
        inner = [inner_edge[s, k] - OBJ_RATE * (in_edge[s, k] + ns_inner[1, s, k]) for k in range(2)]
        for k, value in enumerate(unpack(*packs, inner)):
            out_obj[s, k, :HALO, :] = value[:HALO]
            out_obj[s, k, tile - HALO :, :] = value[HALO:]

    collect_edge(1)
    relay(1, MID)
    relay(0, MID)
    collect_edge(0)
    for held in range(1, rows):
        spread_rows(held)
    collect_mid(1)
    collect_mid(0)
    finish_edge(1)
    finish_edge(0)

    off_near.sent()
    off_far.sent()
    for s in range(2):
        for phase in range(2):
            for link in ns[phase][s][PACK] + ns[phase][s][INNER]:
                link.sent()
        for piece in range(2):
            for group in (far_link, msg_link, gmsg_link, pass_link):
                group[s][piece].sent()
    for copy in row_down + rs_cols + ag_cols + list(row_up.values()):
        copy.wait_send()


def store(obj, probe, part, out_obj, out_probe, out_part, sem):
    copies = [
        pltpu.make_async_copy(src, dst, sem.at[k])
        for k, (src, dst) in enumerate(((obj, out_obj), (probe, out_probe), (part, out_part)))
    ]
    for copy in copies:
        copy.start()
    for copy in copies:
        copy.wait()


def shards(rows, cols, objects, probe, prev_partial, offsets, counts, amplitudes):
    tile = objects.shape[2]
    win = probe.shape[-1]
    assert tile == win == 4 * HALO and cols % 2 == 0
    piece = (2 * win) // (rows * cols)
    split_shape = (rows, cols, piece, win)
    table = jnp.asarray(operator_table(win))
    f32 = jnp.float32
    smem = pl.BlockSpec(memory_space=pltpu.SMEM)
    anyspace = pl.BlockSpec(memory_space=pl.ANY)
    vmem = pl.BlockSpec(memory_space=pltpu.VMEM)
    V = lambda *shape: pltpu.VMEM(shape, f32)
    mid, wide = tile - 2 * HALO, 2 * HALO
    dma = pltpu.SemaphoreType.DMA
    scratch = [
        V(2, 2, tile, tile), V(*split_shape), V(2, win, win), V(piece, win), V(win, win),
        pltpu.VMEM(table.shape, jnp.bfloat16),
        pltpu.VMEM((2, 8, wide), jnp.int32), pltpu.VMEM((2, 2, 8, wide), jnp.int32),
        V(2, 2, mid, wide), V(2, 2, wide, wide), V(2, 2, wide, wide), V(2, 2, 2, wide, wide), V(2, 2, 2, wide, wide),
        V(2, wide, wide),
        V(2, mid, wide), V(2, wide, wide), V(2, mid, wide), V(2, wide, wide), V(2, mid, wide), V(2, wide, wide),
        V(2, 2, tile, tile),
        V(2, mid, wide), V(2, wide, wide), V(2, 2, mid, wide), V(2, 2, wide, wide),
        V(2, 2, wide, wide), V(2, 2, wide, wide), V(2, 2, mid, wide), V(2, 2, wide, wide), V(2, 2, mid, wide), V(2, 2, wide, wide),
        V(max(rows - 1, 1), cols, piece, win), V(max(cols - 1, 1), piece, win),
        dma((7,)), dma((2,)), dma((2,)), dma((2, 2, 4)), dma((2, 2, 4)),
        dma((2, 2, 2)), dma((2, 2, 2)), dma((2, 2, 2)), dma((2, 2, 2)),
        dma((2, max(rows - 1, 1))), dma((2, max(rows - 1, 1))),
        dma((2, max(cols - 1, 1))), dma((2, max(cols - 1, 1))),
        pltpu.SemaphoreType.REGULAR((max(cols.bit_length() - 2, 1),)),
    ]
    results = pl.pallas_call(
        functools.partial(kernel, rows, cols),
        out_shape=(
            pltpu.VMEM(objects.shape, f32), pltpu.VMEM(split_shape, f32), pltpu.VMEM(probe.shape, f32),
        ),
        in_specs=[smem, smem] + [anyspace] * 6,
        out_specs=(vmem, vmem, vmem),
        scratch_shapes=scratch,
        compiler_params=pltpu.CompilerParams(
            collective_id=0, has_side_effects=True, vmem_limit_bytes=56 * 2**20
        ),
    )(
        offsets.reshape(2), counts.reshape(1), objects, prev_partial.reshape(split_shape),
        probe, probe.reshape(split_shape), amplitudes.reshape(win, win), table,
    )
    new_obj, new_probe, part = pl.pallas_call(
        store,
        out_shape=tuple(jax.ShapeDtypeStruct(v.shape, f32) for v in results),
        in_specs=[vmem] * 3,
        out_specs=(pl.BlockSpec(memory_space=pltpu.HBM),) * 3,
        scratch_shapes=[dma((3,))],
    )(*[pltpu.with_memory_space_constraint(v, pltpu.VMEM) for v in results])
    return new_obj, new_probe.reshape(probe.shape), part[None, None]


def solution(mesh):
    in_specs = (
        P(None, None, "row", "col"),
        P(),
        P("row", "col", None, None, None),
        P("row", "col", None, None),
        P("row", "col"),
        P("row", "col", None, None, None),
    )
    out_specs = (P(None, None, "row", "col"), P(), P("row", "col", None, None, None))
    body = functools.partial(shards, mesh.shape["row"], mesh.shape["col"])
    return jax.shard_map(body, mesh=mesh, in_specs=in_specs, out_specs=out_specs, check_vma=False)
```

```python
import functools
import math

import jax
import jax.numpy as jnp
import numpy as np
from jax import lax
from jax.experimental import pallas as pl
from jax.experimental.pallas import tpu as pltpu
from jax.sharding import PartitionSpec as P

HALO = 64
OBJ_RATE = 0.1
PROBE_RATE = 0.3
MESH = pl.DeviceIdType.MESH


def split(value):
    high = value.astype(jnp.bfloat16)
    low = (value - high.astype(jnp.float32)).astype(jnp.bfloat16)
    return high, low


def operator_table(n):
    half = n // 2
    index = np.arange(n)
    dft = np.exp(-2j * np.pi * (np.outer(index, index) % n) / n) / np.sqrt(n)
    freq = np.where(index < half, index, index - n).astype(np.float64)
    phase = np.exp(1j * np.pi * freq * freq / (4.0 * n))
    prop = np.conj(dft) @ (phase[:, None] * dft)
    near, far = prop[:half, :half], prop[:half, half:]
    tables = []
    for mat in (dft[0::2, :half], dft[1::2, :half], (near + far) / 2, (near - far) / 2):
        right = np.block([[mat.real.T, mat.imag.T], [-mat.imag.T, mat.real.T]]).astype(np.float32)
        for part in (right, right.T):
            high = part.astype(jnp.bfloat16)
            tables += [high, (part - high.astype(np.float32)).astype(jnp.bfloat16)]
    return np.stack(tables).reshape(2, 2, 2, 2, n, n)


def dot(left, right):
    return jnp.dot(left, right, preferred_element_type=jnp.float32)


def cat(parts, axis):
    return jnp.concatenate(parts, axis=axis)


def times(data, table, which, side, flip):
    kind = int(flip if side else not flip)
    out = []
    for k in range(2):
        high, low = table[which, k, kind, 0], table[which, k, kind, 1]
        dh, dl = split(data[k])
        if side:
            out.append(dot(cat([dh, dl, dh], 1), cat([high, high, low], 0)))
        else:
            out.append(dot(cat([high, high, low], 1), cat([dh, dl, dh], 0)))
    return out


def halves(value, axis):
    half = value.shape[axis] // 2
    return (value[:half], value[half:]) if axis == 0 else (value[:, :half], value[:, half:])


def transform(re, im, table, which, axis, merge, divide, flip):
    if divide:
        parts = [halves(v, axis) for v in (re, im)]
        data = [cat([a + b for a, b in parts], axis), cat([a - b for a, b in parts], axis)]
    else:
        parts = [halves(v, axis) for v in (re, im)]
        data = [cat([p[0] for p in parts], axis), cat([p[1] for p in parts], axis)]
    even, odd = [halves(v, axis) for v in times(data, table, which, axis, flip)]
    if merge:
        return [cat([a + b, a - b], axis) for a, b in zip(even, odd)]
    return [cat([a, b], axis) for a, b in zip(even, odd)]


def sandwich(xr, xi, table, which, conj):
    divide = which == 1 or not conj
    merge = which == 1 or conj
    tr, ti = transform(xr, xi, table, which, 1, merge, divide, conj)
    return transform(tr, ti, table, which, 0, merge, divide, conj)


def kernel(
    rows, cols, offs_hbm, count_hbm, obj_hbm, prev_hbm, probe_hbm, probe_k_hbm, amp_hbm, table_hbm,
    out_obj, out_probe, out_part,
    obj, prev, probe, probe_piece, amp, table,
    my_off, off,
    strip_mid, strip_edge, inner_edge, ns_pack, ns_inner, fold_far, far_mid, far_edge, msg_mid, msg_edge, got_mid, got_edge, z,
    gmsg_mid, gmsg_edge, gs_mid, gs_edge, pack_out, inner_out, pack_mid, pack_edge, in_mid, in_edge,
    buf1, buf2,
    offs, count, local_sem, off_send, off_recv, ns_send, ns_recv, far_send, far_recv, msg_send, msg_recv,
    row_send, row_recv, col_send, col_recv, known,
):
    tile = obj.shape[2]
    mid_rows = tile - 2 * HALO
    wide = 2 * HALO
    row, col = lax.axis_index("row"), lax.axis_index("col")
    odd = lax.rem(col, 2)
    step = 1 - 2 * odd
    near = 1 - odd
    far = odd
    partner, other = col + step, col - step
    ahead, behind = col + 2 * step, col - 2 * step
    has_other = (other >= 0) & (other < cols)
    has_ahead = (ahead >= 0) & (ahead < cols)
    has_behind = (behind >= 0) & (behind < cols)
    has_north, has_south = row > 0, row < rows - 1
    always = row >= 0

    def flip(value, bit):
        return value + bit * (1 - 2 * lax.rem(value // bit, 2))

    row_bits = [1 << k for k in range(rows.bit_length() - 1)]
    base, length, row_down, row_keep = 0, rows, [], []
    for k, bit in enumerate(row_bits):
        length = length // 2
        upper = lax.rem(row // bit, 2)
        keep, give = base + upper * length, base + (1 - upper) * length
        landing = buf1.at[pl.ds(rows - 2 * length, length)]
        row_down.append(pltpu.make_async_remote_copy(
            src_ref=prev.at[pl.ds(give, length)], dst_ref=landing, send_sem=row_send.at[0, k],
            recv_sem=row_recv.at[0, k], device_id=(flip(row, bit), col), device_id_type=MESH))
        row_keep.append((keep, length, landing))
        base = keep
    slot = base
    row_up = {}
    for k, bit in enumerate(reversed(row_bits)):
        for held in range(1 << k):
            where = slot
            for t in range(k):
                where = flip(where, 1 << t) if held >> t & 1 else where
            here, index = out_probe.at[where], held | 1 << k
            row_up[index] = pltpu.make_async_remote_copy(
                src_ref=here, dst_ref=here, send_sem=row_send.at[1, index - 1],
                recv_sem=row_recv.at[1, index - 1], device_id=(flip(row, bit), col), device_id_type=MESH)

    def spread_rows(held):
        if held:
            row_up[held].wait_recv()
        for k in range(held.bit_length(), len(row_bits)):
            row_up[held | 1 << k].start()

    fetches = [
        pltpu.make_async_copy(src, dst, local_sem.at[k])
        for k, (src, dst) in enumerate(
            ((obj_hbm.at[0], obj.at[0]), (obj_hbm.at[1], obj.at[1]), (prev_hbm, prev),
             (probe_hbm, probe), (probe_k_hbm.at[slot, col], probe_piece),
             (table_hbm, table), (amp_hbm, amp), (offs_hbm, offs), (count_hbm, count))
        )
    ]
    for k in (7, 0, 1, 2):
        fetches[k].start()

    barrier = pltpu.get_barrier_semaphore()

    def greet(sem, r, c):
        pl.semaphore_signal(sem, inc=1, device_id=(r, c), device_id_type=MESH)

    bits = [1 << k for k in range(cols.bit_length() - 1)]
    expected = 0
    for t in range(1, rows):
        greet(barrier, lax.rem(row + t, rows), col)
        expected = expected + 1
    for ok, c in ((always, partner), (has_other, other), (has_ahead, ahead), (has_behind, behind)):
        @pl.when(ok)
        def _():
            greet(barrier, row, c)
        expected = expected + ok.astype(jnp.int32)
    for bit in bits[2:]:
        greet(barrier, row, flip(col, bit))
        expected = expected + 1

    fetches[7].wait()
    top, left = offs[0], offs[1]
    my_off[0] = jnp.zeros((8, wide), jnp.int32) + top
    my_off[1] = jnp.zeros((8, wide), jnp.int32) + left

    lane = lax.broadcasted_iota(jnp.int32, (1, wide), 1)
    first = lane < HALO
    lane64 = jnp.where(first, lane, lane - HALO)
    line = lax.broadcasted_iota(jnp.int32, (wide, 1), 0)

    def swap(value):
        return pltpu.roll(value, HALO, 1)

    def turned(index, corner):
        return (index < corner - HALO) | (index >= corner + HALO)

    def pack(ref, slot):
        re, im = ref
        if slot == 0:
            return jnp.where(first, re[:, :wide], swap(im[:, :wide]))
        return jnp.where(first, swap(re[:, tile - wide :]), im[:, tile - wide :])

    def inner_of(value):
        return jnp.where(first, value[:, wide:], value[:, :wide])

    def unpack(head, tail, inner):
        re = cat([jnp.where(first, head, inner[0]), jnp.where(first, inner[0], swap(tail))], 1)
        im = cat([jnp.where(first, swap(head), inner[1]), jnp.where(first, inner[1], tail)], 1)
        return re, im

    def ends(value):
        return cat([value[:HALO], value[tile - HALO :]], 0)

    class Link:
        def __init__(self, src, dst, send_sem, recv_sem, device, ok, inbound):
            self.copy = pltpu.make_async_remote_copy(
                src_ref=src, dst_ref=dst, send_sem=send_sem, recv_sem=recv_sem,
                device_id=device, device_id_type=MESH)
            self.ok, self.inbound = ok, inbound

        def start(self):
            @pl.when(self.ok)
            def _():
                self.copy.start()

        def arrive(self):
            @pl.when(self.inbound)
            def _():
                self.copy.wait_recv()

        def sent(self):
            @pl.when(self.ok)
            def _():
                self.copy.wait_send()

    up, down = slice(0, HALO), slice(HALO, wide)
    off_near = Link(my_off, off.at[1 - near], off_send.at[0], off_recv.at[0], (row, partner), always, always)
    off_far = Link(my_off, off.at[1 - far], off_send.at[1], off_recv.at[1], (row, other), has_other, has_other)

    north, south = (row - 1, has_north, has_south), (row + 1, has_south, has_north)

    def ns_links(phase, s, kind):
        if kind == 0:
            src = strip_edge.at[:, s] if phase == 0 else pack_out.at[s]
            dst = ns_pack.at[phase, s]
        else:
            src = (inner_edge if phase == 0 else inner_out).at[s]
            dst = ns_inner.at[phase, s]
        made = []
        for k, (span, to) in enumerate(((up, south if phase else north), (down, north if phase else south))):
            sem = 2 * kind + k
            made.append(Link(src.at[:, span, :], dst.at[:, span, :], ns_send.at[phase, s, sem], ns_recv.at[phase, s, sem],
                             (to[0], col), to[1], to[2]))
        return made

    PACK, INNER = 0, 1
    ns = [[[ns_links(phase, s, kind) for kind in range(2)] for s in range(2)] for phase in range(2)]
    MID, EDGE = (0, 1), (2, 3)
    halves_of = (slice(0, HALO), slice(HALO, wide))

    def chunks(make):
        return [[make(s, p, p // 2, halves_of[p % 2]) for p in range(4)] for s in range(2)]

    far_link = chunks(lambda s, p, b, rows_: Link(
        fold_far.at[s, rows_] if b else strip_mid.at[far, s, rows_], (far_mid, far_edge)[b].at[s, rows_],
        far_send.at[0, s, p], far_recv.at[0, s, p], (row, behind), has_behind, has_ahead))
    msg_link = chunks(lambda s, p, b, rows_: Link(
        (msg_mid, msg_edge)[b].at[s, rows_], (got_mid, got_edge)[b].at[s, rows_],
        msg_send.at[0, s, p], msg_recv.at[0, s, p], (row, partner), always, always))
    gmsg_link = chunks(lambda s, p, b, rows_: Link(
        (gmsg_mid, gmsg_edge)[b].at[s, rows_], (gs_mid, gs_edge)[b].at[1 - near, s, rows_],
        msg_send.at[1, s, p], msg_recv.at[1, s, p], (row, partner), always, always))
    pass_link = chunks(lambda s, p, b, rows_: Link(
        (gs_mid, gs_edge)[b].at[near, s, rows_], (gs_mid, gs_edge)[b].at[far, s, rows_],
        far_send.at[1, s, p], far_recv.at[1, s, p], (row, ahead), has_ahead, has_behind))

    def start(links, pieces):
        for p in pieces:
            links[p].start()

    def arrive(links, pieces):
        for p in pieces:
            links[p].arrive()

    def add_rows(k):
        keep, count_rows, landing = row_keep[k]
        row_down[k].wait_recv()
        prev[pl.ds(keep, count_rows)] += landing[...]

    def col_copies(stage):
        made = []
        for t in range(1, cols):
            peer = lax.rem(col + t, cols)
            if stage == 0:
                src, dst = prev.at[slot, peer], buf2.at[t - 1]
            else:
                src, dst = out_probe.at[slot, col], out_probe.at[slot, col]
            made.append(pltpu.make_async_remote_copy(
                src_ref=src, dst_ref=dst, send_sem=col_send.at[stage, t - 1],
                recv_sem=col_recv.at[stage, t - 1], device_id=(row, peer), device_id_type=MESH))
        return made

    def pack_slice(s):
        fetches[s].wait()
        for side in range(2):
            value = pack((obj[s, 0], obj[s, 1]), side)
            strip_mid[side, s] = value[HALO : tile - HALO]
            strip_edge[side, s] = ends(value)

    pack_slice(0)
    pl.semaphore_wait(barrier, expected)
    off_near.start()
    off_far.start()
    for link in ns[0][0][PACK]:
        link.start()
    start(far_link[0], MID)
    pack_slice(1)
    for link in ns[0][1][PACK]:
        link.start()
    start(far_link[1], MID)
    fetches[2].wait()
    row_down[0].start()
    for s in range(2):
        for k in range(2):
            inner_edge[s, k] = inner_of(ends(obj[s, k]))
        for link in ns[0][s][INNER]:
            link.start()
    for bit in bits:
        greet(known.at[0], row, flip(col, bit))
    for k in (3, 4, 5, 6, 8):
        fetches[k].start()

    @pl.when(jnp.logical_not(has_other))
    def _():
        off[far] = jnp.full((2, 8, wide), HALO, jnp.int32)

    for s in range(2):
        for phase, spans in ((0, ((has_south, slice(0, HALO)), (has_north, slice(HALO, wide)))),
                             (1, ((has_north, slice(0, HALO)), (has_south, slice(HALO, wide))))):
            for ok, span in spans:
                @pl.when(jnp.logical_not(ok))
                def _():
                    ns_pack[phase, s, :, span, :] = jnp.zeros((2, HALO, wide), jnp.float32)
                    ns_inner[phase, s, :, span, :] = jnp.zeros((2, HALO, wide), jnp.float32)

        @pl.when(jnp.logical_not(has_ahead))
        def _():
            far_mid[s] = jnp.zeros((mid_rows, wide), jnp.float32)
            far_edge[s] = jnp.zeros((wide, wide), jnp.float32)

        @pl.when(jnp.logical_not(has_behind))
        def _():
            gs_mid[far, s] = jnp.zeros((mid_rows, wide), jnp.float32)
            gs_edge[far, s] = jnp.zeros((wide, wide), jnp.float32)

    fetches[3].wait()
    turn_rows = lax.rem(top + tile - HALO, tile)
    turn_cols = lax.rem(left + tile - HALO, tile)
    for k in range(2):
        probe[k] = pltpu.roll(pltpu.roll(probe[k], turn_rows, 0), turn_cols, 1)

    fetches[6].wait()
    count_half = tile // 2

    def order(axis):
        target = lax.broadcasted_iota(jnp.int32, (tile, tile), axis)
        source = lax.broadcasted_iota(jnp.int32, (tile, tile), 1 - axis)
        target = jnp.where(target < count_half, 2 * target, 2 * (target - count_half) + 1)
        return (source == target).astype(jnp.float32).astype(jnp.bfloat16)

    ordered = dot(cat([order(0), order(0)], 1), cat(split(amp[...]), 0))
    amp[...] = dot(cat(split(ordered), 1), cat([order(1), order(1)], 0))

    off_near.arrive()
    off_far.arrive()
    near_off, far_off = off[near], off[far]
    near_top, near_left = near_off[0, :1], near_off[1, :1]
    far_top = far_off[0, :1]
    take_own = jnp.where(near == 0, near_left - HALO, HALO - near_left) > 0

    def fold(s):
        for h, rows_ in enumerate(halves_of):
            ns[0][s][PACK][h].arrive()
            fold_far[s, rows_] = jnp.where(turned(line[rows_], far_top), ns_pack[0, s, far, rows_], strip_edge[far, s, rows_])
            far_link[s][EDGE[h]].start()
        for rows_ in halves_of:
            msg_edge[s, rows_] = jnp.where(turned(line[rows_], near_top), ns_pack[0, s, near, rows_], strip_edge[near, s, rows_])

    def forward_mid(s):
        for p, rows_ in zip(MID, halves_of):
            far_link[s][p].arrive()
            msg_mid[s, rows_] = jnp.where(take_own, strip_mid[near, s, rows_], far_mid[s, rows_])
            msg_link[s][p].start()

    def forward_edge(s):
        for p, rows_ in zip(EDGE, halves_of):
            far_link[s][p].arrive()
            msg_edge[s, rows_] = jnp.where(take_own, msg_edge[s, rows_], far_edge[s, rows_])
            msg_link[s][p].start()

    add_rows(0)
    for k in range(1, len(row_bits)):
        row_down[k].start()
        if k + 1 < len(row_bits):
            add_rows(k)
    fold(0)
    forward_mid(0)
    fold(1)
    forward_mid(1)
    forward_edge(0)
    forward_edge(1)

    for wait_round, bit in enumerate(bits[1:]):
        pl.semaphore_wait(known.at[wait_round], len(bits))
        if wait_round + 1 < len(bits) - 1:
            for again in bits:
                greet(known.at[wait_round + 1], row, flip(col, again))

    def assemble(s):
        from_east, from_west = lane64 < left - HALO, lane64 >= left

        arrive(msg_link[s], MID)
        packs = [jnp.where(take, got_mid[s], strip_mid[side, s]) for side, take in enumerate((from_east, from_west))]
        inner = [inner_of(obj[s, k, HALO : tile - HALO, :]) for k in range(2)]
        for k, value in enumerate(unpack(*packs, inner)):
            z[s, k, HALO : tile - HALO, :] = value
        for link in ns[0][s][INNER]:
            link.arrive()
        away = turned(line, top)
        inner = [jnp.where(away, ns_inner[0, s, k], inner_edge[s, k]) for k in range(2)]
        packs = [jnp.where(away, ns_pack[0, s, side], strip_edge[side, s]) for side in range(2)]
        arrive(msg_link[s], EDGE)
        packs = [jnp.where(take, got_edge[s], packs[side]) for side, take in enumerate((from_east, from_west))]
        for k, value in enumerate(unpack(*packs, inner)):
            z[s, k, :HALO, :] = value[:HALO]
            z[s, k, tile - HALO :, :] = value[HALO:]

    def back(s, gre, gim):
        leaves = lane64 < left - HALO, lane64 >= left
        packs = [pack((gre, gim), side) for side in range(2)]
        out = [jnp.where(leave, value, 0.0) for leave, value in zip(leaves, packs)]
        value = jnp.where(left > HALO, out[0], out[1])
        gmsg_edge[s] = ends(value)
        start(gmsg_link[s], EDGE)
        gmsg_mid[s] = value[HALO : tile - HALO]
        if s == 0:
            start(gmsg_link[1], MID)
            start(gmsg_link[0], MID)
        away = turned(line, top)
        inner = [inner_of(grad) for grad in (gre, gim)]
        for k in range(2):
            edge = ends(inner[k])
            inner_out[s, k] = jnp.where(away, edge, 0.0)
            in_edge[s, k] = jnp.where(away, 0.0, edge)
        for link in ns[1][s][INNER]:
            link.start()
        for k in range(2):
            in_mid[s, k] = inner[k][HALO : tile - HALO]
            stay = jnp.where(leaves[k], 0.0, packs[k])
            pack_mid[s, k] = stay[HALO : tile - HALO]
            edge = ends(stay)
            pack_out[s, k] = jnp.where(away, edge, 0.0)
            pack_edge[s, k] = jnp.where(away, 0.0, edge)

    if len(row_bits) > 1:
        add_rows(len(row_bits) - 1)
    rs_cols = col_copies(0)
    for copy in rs_cols:
        copy.start()

    fetches[5].wait()
    assemble(0)
    ar, ai = z[0, 0], z[0, 1]
    pr, pi = probe[0], probe[1]
    vr, vi = sandwich(pr * ar - pi * ai, pr * ai + pi * ar, table, 1, False)

    assemble(1)
    br, bi = z[1, 0], z[1, 1]
    wr, wi = sandwich(vr * br - vi * bi, vr * bi + vi * br, table, 0, False)
    fetches[8].wait()
    live = jnp.where(count[0] > 0, 2.0, 0.0)
    scale = live - (live * amp[...]) * lax.rsqrt(wr * wr + wi * wi + 1.0)
    xr, xi = sandwich(scale * wr, scale * wi, table, 0, True)
    back(1, xr * vr + xi * vi, xi * vr - xr * vi)

    for copy in rs_cols:
        copy.wait_recv()
    fetches[4].wait()
    total = prev[slot, col]
    for t in range(1, cols):
        total = total + buf2[t - 1]
    rate = PROBE_RATE / math.sqrt(rows * cols)
    out_probe[slot, col] = probe_piece[...] - rate * total
    ag_cols = col_copies(1)
    for copy in ag_cols:
        copy.start()


    ur, ui = sandwich(xr * br + xi * bi, xi * br - xr * bi, table, 1, True)
    back(0, ur * pr + ui * pi, ui * pr - ur * pi)

    def relay(s, pieces):
        for p in pieces:
            gmsg_link[s][p].arrive()
            pass_link[s][p].start()

    relay(1, EDGE)
    for copy in ag_cols:
        copy.wait_recv()
    spread_rows(0)
    relay(0, EDGE)
    home_rows = lax.rem(tile + HALO - top, tile)
    home_cols = lax.rem(tile + HALO - left, tile)
    out_part[0] = pltpu.roll(pltpu.roll(ur * ar + ui * ai, home_rows, 0), home_cols, 1)
    out_part[1] = pltpu.roll(pltpu.roll(ui * ar - ur * ai, home_rows, 0), home_cols, 1)

    head_off, tail_off = off[0], off[1]
    accept = (head_off[1, :1] > HALO, tail_off[1, :1] < HALO)
    corner = (head_off[0, :1], tail_off[0, :1])

    def collect_edge(s):
        for h, rows_ in enumerate(halves_of):
            pass_link[s][EDGE[h]].arrive()
            kept = []
            for side in range(2):
                strip = jnp.where(accept[side], gs_edge[side, s, rows_], 0.0)
                moves = turned(line[rows_], corner[side])
                pack_out[s, side, rows_] += jnp.where(moves, strip, 0.0)
                kept.append(jnp.where(moves, 0.0, strip))
            ns[1][s][PACK][h].start()
            for side in range(2):
                pack_edge[s, side, rows_] += kept[side]

    def collect_mid(s):
        arrive(pass_link[s], MID)
        packs = [
            strip_mid[side, s] - OBJ_RATE * (pack_mid[s, side] + jnp.where(accept[side], gs_mid[side, s], 0.0))
            for side in range(2)
        ]
        inner = [inner_of(obj[s, k, HALO : tile - HALO, :]) - OBJ_RATE * in_mid[s, k] for k in range(2)]
        for k, value in enumerate(unpack(*packs, inner)):
            out_obj[s, k, HALO : tile - HALO, :] = value

    def finish_edge(s):
        for kind in (INNER, PACK):
            for link in ns[1][s][kind]:
                link.arrive()
        packs = [strip_edge[side, s] - OBJ_RATE * (pack_edge[s, side] + ns_pack[1, s, side]) for side in range(2)]
        inner = [inner_edge[s, k] - OBJ_RATE * (in_edge[s, k] + ns_inner[1, s, k]) for k in range(2)]
        for k, value in enumerate(unpack(*packs, inner)):
            out_obj[s, k, :HALO, :] = value[:HALO]
            out_obj[s, k, tile - HALO :, :] = value[HALO:]

    collect_edge(1)
    relay(1, MID)
    relay(0, MID)
    collect_edge(0)
    for held in range(1, rows):
        spread_rows(held)
    collect_mid(1)
    collect_mid(0)
    finish_edge(1)
    finish_edge(0)

    off_near.sent()
    off_far.sent()
    for s in range(2):
        for phase in range(2):
            for link in ns[phase][s][PACK] + ns[phase][s][INNER]:
                link.sent()
        for piece in range(4):
            for group in (far_link, msg_link, gmsg_link, pass_link):
                group[s][piece].sent()
    for copy in row_down + rs_cols + ag_cols + list(row_up.values()):
        copy.wait_send()


def store(obj, probe, part, out_obj, out_probe, out_part, sem):
    copies = [
        pltpu.make_async_copy(src, dst, sem.at[k])
        for k, (src, dst) in enumerate(((obj, out_obj), (probe, out_probe), (part, out_part)))
    ]
    for copy in copies:
        copy.start()
    for copy in copies:
        copy.wait()


def shards(rows, cols, objects, probe, prev_partial, offsets, counts, amplitudes):
    tile = objects.shape[2]
    win = probe.shape[-1]
    assert tile == win == 4 * HALO and cols % 2 == 0
    piece = (2 * win) // (rows * cols)
    split_shape = (rows, cols, piece, win)
    table = jnp.asarray(operator_table(win))
    f32 = jnp.float32
    anyspace = pl.BlockSpec(memory_space=pl.ANY)
    vmem = pl.BlockSpec(memory_space=pltpu.VMEM)
    V = lambda *shape: pltpu.VMEM(shape, f32)
    mid, wide = tile - 2 * HALO, 2 * HALO
    dma = pltpu.SemaphoreType.DMA
    scratch = [
        V(2, 2, tile, tile), V(*split_shape), V(2, win, win), V(piece, win), V(win, win),
        pltpu.VMEM(table.shape, jnp.bfloat16),
        pltpu.VMEM((2, 8, wide), jnp.int32), pltpu.VMEM((2, 2, 8, wide), jnp.int32),
        V(2, 2, mid, wide), V(2, 2, wide, wide), V(2, 2, wide, wide), V(2, 2, 2, wide, wide), V(2, 2, 2, wide, wide),
        V(2, wide, wide),
        V(2, mid, wide), V(2, wide, wide), V(2, mid, wide), V(2, wide, wide), V(2, mid, wide), V(2, wide, wide),
        V(2, 2, tile, tile),
        V(2, mid, wide), V(2, wide, wide), V(2, 2, mid, wide), V(2, 2, wide, wide),
        V(2, 2, wide, wide), V(2, 2, wide, wide), V(2, 2, mid, wide), V(2, 2, wide, wide), V(2, 2, mid, wide), V(2, 2, wide, wide),
        V(max(rows - 1, 1), cols, piece, win), V(max(cols - 1, 1), piece, win),
        pltpu.SMEM((2,), jnp.int32), pltpu.SMEM((1,), jnp.int32), dma((9,)), dma((2,)), dma((2,)), dma((2, 2, 4)), dma((2, 2, 4)),
        dma((2, 2, 4)), dma((2, 2, 4)), dma((2, 2, 4)), dma((2, 2, 4)),
        dma((2, max(rows - 1, 1))), dma((2, max(rows - 1, 1))),
        dma((2, max(cols - 1, 1))), dma((2, max(cols - 1, 1))),
        pltpu.SemaphoreType.REGULAR((max(cols.bit_length() - 2, 1),)),
    ]
    results = pl.pallas_call(
        functools.partial(kernel, rows, cols),
        out_shape=(
            pltpu.VMEM(objects.shape, f32), pltpu.VMEM(split_shape, f32), pltpu.VMEM(probe.shape, f32),
        ),
        in_specs=[anyspace] * 8,
        out_specs=(vmem, vmem, vmem),
        scratch_shapes=scratch,
        compiler_params=pltpu.CompilerParams(
            collective_id=0, has_side_effects=True, vmem_limit_bytes=56 * 2**20
        ),
    )(
        offsets.reshape(2), counts.reshape(1), objects, prev_partial.reshape(split_shape),
        probe, probe.reshape(split_shape), amplitudes.reshape(win, win), table,
    )
    new_obj, new_probe, part = pl.pallas_call(
        store,
        out_shape=tuple(jax.ShapeDtypeStruct(v.shape, f32) for v in results),
        in_specs=[vmem] * 3,
        out_specs=(pl.BlockSpec(memory_space=pltpu.HBM),) * 3,
        scratch_shapes=[dma((3,))],
    )(*[pltpu.with_memory_space_constraint(v, pltpu.VMEM) for v in results])
    return new_obj, new_probe.reshape(probe.shape), part[None, None]


def solution(mesh):
    in_specs = (
        P(None, None, "row", "col"),
        P(),
        P("row", "col", None, None, None),
        P("row", "col", None, None),
        P("row", "col"),
        P("row", "col", None, None, None),
    )
    out_specs = (P(None, None, "row", "col"), P(), P("row", "col", None, None, None))
    body = functools.partial(shards, mesh.shape["row"], mesh.shape["col"])
    return jax.shard_map(body, mesh=mesh, in_specs=in_specs, out_specs=out_specs, check_vma=False)
```

```python
import functools
import math

import jax
import jax.numpy as jnp
import numpy as np
from jax import lax
from jax.experimental import pallas as pl
from jax.experimental.pallas import tpu as pltpu
from jax.sharding import PartitionSpec as P

HALO = 64
OBJ_RATE = 0.1
PROBE_RATE = 0.3
MESH = pl.DeviceIdType.MESH


def split(value):
    high = value.astype(jnp.bfloat16)
    low = (value - high.astype(jnp.float32)).astype(jnp.bfloat16)
    return high, low


def operator_table(n):
    half = n // 2
    index = np.arange(n)
    dft = np.exp(-2j * np.pi * (np.outer(index, index) % n) / n) / np.sqrt(n)
    freq = np.where(index < half, index, index - n).astype(np.float64)
    phase = np.exp(1j * np.pi * freq * freq / (4.0 * n))
    prop = np.conj(dft) @ (phase[:, None] * dft)
    near, far = prop[:half, :half], prop[:half, half:]
    tables = []
    for mat in (dft[0::2, :half], dft[1::2, :half], (near + far) / 2, (near - far) / 2):
        right = np.block([[mat.real.T, mat.imag.T], [-mat.imag.T, mat.real.T]]).astype(np.float32)
        for part in (right, right.T):
            high = part.astype(jnp.bfloat16)
            tables += [high, (part - high.astype(np.float32)).astype(jnp.bfloat16)]
    return np.stack(tables).reshape(2, 2, 2, 2, n, n)


def dot(left, right):
    return jnp.dot(left, right, preferred_element_type=jnp.float32)


def cat(parts, axis):
    return jnp.concatenate(parts, axis=axis)


def times(data, table, which, side, flip):
    kind = int(flip if side else not flip)
    out = []
    for k in range(2):
        high, low = table[which, k, kind, 0], table[which, k, kind, 1]
        dh, dl = split(data[k])
        if side:
            out.append(dot(cat([dh, dl, dh], 1), cat([high, high, low], 0)))
        else:
            out.append(dot(cat([high, high, low], 1), cat([dh, dl, dh], 0)))
    return out


def halves(value, axis):
    half = value.shape[axis] // 2
    return (value[:half], value[half:]) if axis == 0 else (value[:, :half], value[:, half:])


def transform(re, im, table, which, axis, merge, divide, flip):
    if divide:
        parts = [halves(v, axis) for v in (re, im)]
        data = [cat([a + b for a, b in parts], axis), cat([a - b for a, b in parts], axis)]
    else:
        parts = [halves(v, axis) for v in (re, im)]
        data = [cat([p[0] for p in parts], axis), cat([p[1] for p in parts], axis)]
    even, odd = [halves(v, axis) for v in times(data, table, which, axis, flip)]
    if merge:
        return [cat([a + b, a - b], axis) for a, b in zip(even, odd)]
    return [cat([a, b], axis) for a, b in zip(even, odd)]


def sandwich(xr, xi, table, which, conj):
    divide = which == 1 or not conj
    merge = which == 1 or conj
    tr, ti = transform(xr, xi, table, which, 1, merge, divide, conj)
    return transform(tr, ti, table, which, 0, merge, divide, conj)


def kernel(
    rows, cols, offs_hbm, count_hbm, obj_hbm, prev_hbm, probe_hbm, probe_k_hbm, amp_hbm, table_hbm,
    out_obj, out_probe, out_part,
    obj, prev, probe, probe_piece, amp, table,
    my_off, off,
    strip_mid, strip_edge, inner_edge, ns_pack, ns_inner, fold_far, far_mid, far_edge, msg_mid, msg_edge, got_mid, got_edge, z,
    gmsg_mid, gmsg_edge, gs_mid, gs_edge, pack_out, inner_out, pack_mid, pack_edge, in_mid, in_edge,
    buf1, buf2,
    offs, count, local_sem, off_send, off_recv, ns_send, ns_recv, far_send, far_recv, msg_send, msg_recv,
    row_send, row_recv, col_send, col_recv, known,
):
    tile = obj.shape[2]
    mid_rows = tile - 2 * HALO
    wide = 2 * HALO
    row, col = lax.axis_index("row"), lax.axis_index("col")
    odd = lax.rem(col, 2)
    step = 1 - 2 * odd
    near = 1 - odd
    far = odd
    partner, other = col + step, col - step
    ahead, behind = col + 2 * step, col - 2 * step
    has_other = (other >= 0) & (other < cols)
    has_ahead = (ahead >= 0) & (ahead < cols)
    has_behind = (behind >= 0) & (behind < cols)
    has_north, has_south = row > 0, row < rows - 1
    always = row >= 0

    def flip(value, bit):
        return value + bit * (1 - 2 * lax.rem(value // bit, 2))

    row_bits = [1 << k for k in range(rows.bit_length() - 1)]
    base, length, row_down, row_keep = 0, rows, [], []
    for k, bit in enumerate(row_bits):
        length = length // 2
        upper = lax.rem(row // bit, 2)
        keep, give = base + upper * length, base + (1 - upper) * length
        landing = buf1.at[pl.ds(rows - 2 * length, length)]
        row_down.append(pltpu.make_async_remote_copy(
            src_ref=prev.at[pl.ds(give, length)], dst_ref=landing, send_sem=row_send.at[0, k],
            recv_sem=row_recv.at[0, k], device_id=(flip(row, bit), col), device_id_type=MESH))
        row_keep.append((keep, length, landing))
        base = keep
    slot = base
    row_up = {}
    for k, bit in enumerate(reversed(row_bits)):
        for held in range(1 << k):
            where = slot
            for t in range(k):
                where = flip(where, 1 << t) if held >> t & 1 else where
            here, index = out_probe.at[where], held | 1 << k
            row_up[index] = pltpu.make_async_remote_copy(
                src_ref=here, dst_ref=here, send_sem=row_send.at[1, index - 1],
                recv_sem=row_recv.at[1, index - 1], device_id=(flip(row, bit), col), device_id_type=MESH)

    def spread_rows(held):
        if held:
            row_up[held].wait_recv()
        for k in range(held.bit_length(), len(row_bits)):
            row_up[held | 1 << k].start()

    fetches = [
        pltpu.make_async_copy(src, dst, local_sem.at[k])
        for k, (src, dst) in enumerate(
            ((obj_hbm.at[0], obj.at[0]), (obj_hbm.at[1], obj.at[1]), (prev_hbm, prev),
             (probe_hbm, probe), (probe_k_hbm.at[slot, col], probe_piece),
             (table_hbm, table), (amp_hbm, amp), (offs_hbm, offs), (count_hbm, count))
        )
    ]
    for k in (7, 0, 1, 2):
        fetches[k].start()

    barrier = pltpu.get_barrier_semaphore()

    def greet(sem, r, c):
        pl.semaphore_signal(sem, inc=1, device_id=(r, c), device_id_type=MESH)

    bits = [1 << k for k in range(cols.bit_length() - 1)]
    expected = 0
    for t in range(1, rows):
        greet(barrier, lax.rem(row + t, rows), col)
        expected = expected + 1
    for ok, c in ((always, partner), (has_other, other), (has_ahead, ahead), (has_behind, behind)):
        @pl.when(ok)
        def _():
            greet(barrier, row, c)
        expected = expected + ok.astype(jnp.int32)
    for bit in bits[2:]:
        greet(barrier, row, flip(col, bit))
        expected = expected + 1

    fetches[7].wait()
    top, left = offs[0], offs[1]
    my_off[0] = jnp.zeros((8, wide), jnp.int32) + top
    my_off[1] = jnp.zeros((8, wide), jnp.int32) + left

    lane = lax.broadcasted_iota(jnp.int32, (1, wide), 1)
    first = lane < HALO
    lane64 = jnp.where(first, lane, lane - HALO)
    line = lax.broadcasted_iota(jnp.int32, (wide, 1), 0)

    def swap(value):
        return pltpu.roll(value, HALO, 1)

    def turned(index, corner):
        return (index < corner - HALO) | (index >= corner + HALO)

    def pack(ref, slot):
        re, im = ref
        if slot == 0:
            return jnp.where(first, re[:, :wide], swap(im[:, :wide]))
        return jnp.where(first, swap(re[:, tile - wide :]), im[:, tile - wide :])

    def inner_of(value):
        return jnp.where(first, value[:, wide:], value[:, :wide])

    def unpack(head, tail, inner):
        re = cat([jnp.where(first, head, inner[0]), jnp.where(first, inner[0], swap(tail))], 1)
        im = cat([jnp.where(first, swap(head), inner[1]), jnp.where(first, inner[1], tail)], 1)
        return re, im

    def ends(value):
        return cat([value[:HALO], value[tile - HALO :]], 0)

    class Link:
        def __init__(self, src, dst, send_sem, recv_sem, device, ok, inbound):
            self.copy = pltpu.make_async_remote_copy(
                src_ref=src, dst_ref=dst, send_sem=send_sem, recv_sem=recv_sem,
                device_id=device, device_id_type=MESH)
            self.ok, self.inbound = ok, inbound

        def start(self):
            @pl.when(self.ok)
            def _():
                self.copy.start()

        def arrive(self):
            @pl.when(self.inbound)
            def _():
                self.copy.wait_recv()

        def sent(self):
            @pl.when(self.ok)
            def _():
                self.copy.wait_send()

    up, down = slice(0, HALO), slice(HALO, wide)
    off_near = Link(my_off, off.at[1 - near], off_send.at[0], off_recv.at[0], (row, partner), always, always)
    off_far = Link(my_off, off.at[1 - far], off_send.at[1], off_recv.at[1], (row, other), has_other, has_other)

    north, south = (row - 1, has_north, has_south), (row + 1, has_south, has_north)

    def ns_links(phase, s, kind):
        if kind == 0:
            src = strip_edge.at[:, s] if phase == 0 else pack_out.at[s]
            dst = ns_pack.at[phase, s]
        else:
            src = (inner_edge if phase == 0 else inner_out).at[s]
            dst = ns_inner.at[phase, s]
        made = []
        for k, (span, to) in enumerate(((up, south if phase else north), (down, north if phase else south))):
            sem = 2 * kind + k
            made.append(Link(src.at[:, span, :], dst.at[:, span, :], ns_send.at[phase, s, sem], ns_recv.at[phase, s, sem],
                             (to[0], col), to[1], to[2]))
        return made

    PACK, INNER = 0, 1
    ns = [[[ns_links(phase, s, kind) for kind in range(2)] for s in range(2)] for phase in range(2)]
    MID, EDGE = (0, 1), (2, 3)
    halves_of = (slice(0, HALO), slice(HALO, wide))

    def chunks(make):
        return [[make(s, p, p // 2, halves_of[p % 2]) for p in range(4)] for s in range(2)]

    far_link = chunks(lambda s, p, b, rows_: Link(
        fold_far.at[s, rows_] if b else strip_mid.at[far, s, rows_], (far_mid, far_edge)[b].at[s, rows_],
        far_send.at[0, s, p], far_recv.at[0, s, p], (row, behind), has_behind, has_ahead))
    msg_link = chunks(lambda s, p, b, rows_: Link(
        (msg_mid, msg_edge)[b].at[s, rows_], (got_mid, got_edge)[b].at[s, rows_],
        msg_send.at[0, s, p], msg_recv.at[0, s, p], (row, partner), always, always))
    gmsg_link = chunks(lambda s, p, b, rows_: Link(
        (gmsg_mid, gmsg_edge)[b].at[s, rows_], (gs_mid, gs_edge)[b].at[1 - near, s, rows_],
        msg_send.at[1, s, p], msg_recv.at[1, s, p], (row, partner), always, always))
    pass_link = chunks(lambda s, p, b, rows_: Link(
        (gs_mid, gs_edge)[b].at[near, s, rows_], (gs_mid, gs_edge)[b].at[far, s, rows_],
        far_send.at[1, s, p], far_recv.at[1, s, p], (row, ahead), has_ahead, has_behind))

    def start(links, pieces):
        for p in pieces:
            links[p].start()

    def arrive(links, pieces):
        for p in pieces:
            links[p].arrive()

    def add_rows(k):
        keep, count_rows, landing = row_keep[k]
        row_down[k].wait_recv()
        prev[pl.ds(keep, count_rows)] += landing[...]

    def col_copies(stage):
        made = []
        for t in range(1, cols):
            peer = lax.rem(col + t, cols)
            if stage == 0:
                src, dst = prev.at[slot, peer], buf2.at[t - 1]
            else:
                src, dst = out_probe.at[slot, col], out_probe.at[slot, col]
            made.append(pltpu.make_async_remote_copy(
                src_ref=src, dst_ref=dst, send_sem=col_send.at[stage, t - 1],
                recv_sem=col_recv.at[stage, t - 1], device_id=(row, peer), device_id_type=MESH))
        return made

    def pack_slice(s):
        fetches[s].wait()
        for side in range(2):
            value = pack((obj[s, 0], obj[s, 1]), side)
            strip_mid[side, s] = value[HALO : tile - HALO]
            strip_edge[side, s] = ends(value)

    pack_slice(0)
    pl.semaphore_wait(barrier, expected)
    off_near.start()
    off_far.start()
    for link in ns[0][0][PACK]:
        link.start()
    start(far_link[0], MID)
    fetches[2].wait()
    row_down[0].start()
    pack_slice(1)
    for link in ns[0][1][PACK]:
        link.start()
    start(far_link[1], MID)
    for bit in bits:
        greet(known.at[0], row, flip(col, bit))
    for k in (3, 4, 5, 6, 8):
        fetches[k].start()

    @pl.when(jnp.logical_not(has_other))
    def _():
        off[far] = jnp.full((2, 8, wide), HALO, jnp.int32)

    for s in range(2):
        for phase, spans in ((0, ((has_south, slice(0, HALO)), (has_north, slice(HALO, wide)))),
                             (1, ((has_north, slice(0, HALO)), (has_south, slice(HALO, wide))))):
            for ok, span in spans:
                @pl.when(jnp.logical_not(ok))
                def _():
                    ns_pack[phase, s, :, span, :] = jnp.zeros((2, HALO, wide), jnp.float32)
                    ns_inner[phase, s, :, span, :] = jnp.zeros((2, HALO, wide), jnp.float32)

        @pl.when(jnp.logical_not(has_ahead))
        def _():
            far_mid[s] = jnp.zeros((mid_rows, wide), jnp.float32)
            far_edge[s] = jnp.zeros((wide, wide), jnp.float32)

        @pl.when(jnp.logical_not(has_behind))
        def _():
            gs_mid[far, s] = jnp.zeros((mid_rows, wide), jnp.float32)
            gs_edge[far, s] = jnp.zeros((wide, wide), jnp.float32)

    off_near.arrive()
    off_far.arrive()
    near_off, far_off = off[near], off[far]
    near_top, near_left = near_off[0, :1], near_off[1, :1]
    far_top = far_off[0, :1]
    take_own = jnp.where(near == 0, near_left - HALO, HALO - near_left) > 0

    def fold(s):
        for h, rows_ in enumerate(halves_of):
            ns[0][s][PACK][h].arrive()
            fold_far[s, rows_] = jnp.where(turned(line[rows_], far_top), ns_pack[0, s, far, rows_], strip_edge[far, s, rows_])
            far_link[s][EDGE[h]].start()
        for rows_ in halves_of:
            msg_edge[s, rows_] = jnp.where(turned(line[rows_], near_top), ns_pack[0, s, near, rows_], strip_edge[near, s, rows_])

    def forward_mid(s):
        for p, rows_ in zip(MID, halves_of):
            far_link[s][p].arrive()
            msg_mid[s, rows_] = jnp.where(take_own, strip_mid[near, s, rows_], far_mid[s, rows_])
            msg_link[s][p].start()

    def forward_edge(s):
        for p, rows_ in zip(EDGE, halves_of):
            far_link[s][p].arrive()
            msg_edge[s, rows_] = jnp.where(take_own, msg_edge[s, rows_], far_edge[s, rows_])
            msg_link[s][p].start()

    add_rows(0)
    for k in range(1, len(row_bits)):
        row_down[k].start()
        if k + 1 < len(row_bits):
            add_rows(k)
    for s in range(2):
        for k in range(2):
            inner_edge[s, k] = inner_of(ends(obj[s, k]))
        for link in ns[0][s][INNER]:
            link.start()
    fold(0)
    forward_mid(0)
    fold(1)
    forward_mid(1)
    fetches[3].wait()
    turn_rows = lax.rem(top + tile - HALO, tile)
    turn_cols = lax.rem(left + tile - HALO, tile)
    for k in range(2):
        probe[k] = pltpu.roll(pltpu.roll(probe[k], turn_rows, 0), turn_cols, 1)

    fetches[6].wait()
    count_half = tile // 2

    def order(axis):
        target = lax.broadcasted_iota(jnp.int32, (tile, tile), axis)
        source = lax.broadcasted_iota(jnp.int32, (tile, tile), 1 - axis)
        target = jnp.where(target < count_half, 2 * target, 2 * (target - count_half) + 1)
        return (source == target).astype(jnp.float32).astype(jnp.bfloat16)

    ordered = dot(cat([order(0), order(0)], 1), cat(split(amp[...]), 0))
    amp[...] = dot(cat(split(ordered), 1), cat([order(1), order(1)], 0))

    forward_edge(0)
    forward_edge(1)

    for wait_round, bit in enumerate(bits[1:]):
        pl.semaphore_wait(known.at[wait_round], len(bits))
        if wait_round + 1 < len(bits) - 1:
            for again in bits:
                greet(known.at[wait_round + 1], row, flip(col, again))

    def assemble(s):
        from_east, from_west = lane64 < left - HALO, lane64 >= left

        arrive(msg_link[s], MID)
        packs = [jnp.where(take, got_mid[s], strip_mid[side, s]) for side, take in enumerate((from_east, from_west))]
        inner = [inner_of(obj[s, k, HALO : tile - HALO, :]) for k in range(2)]
        for k, value in enumerate(unpack(*packs, inner)):
            z[s, k, HALO : tile - HALO, :] = value
        for link in ns[0][s][INNER]:
            link.arrive()
        away = turned(line, top)
        inner = [jnp.where(away, ns_inner[0, s, k], inner_edge[s, k]) for k in range(2)]
        packs = [jnp.where(away, ns_pack[0, s, side], strip_edge[side, s]) for side in range(2)]
        arrive(msg_link[s], EDGE)
        packs = [jnp.where(take, got_edge[s], packs[side]) for side, take in enumerate((from_east, from_west))]
        for k, value in enumerate(unpack(*packs, inner)):
            z[s, k, :HALO, :] = value[:HALO]
            z[s, k, tile - HALO :, :] = value[HALO:]

    def back(s, edge, middle):
        leaves = lane64 < left - HALO, lane64 >= left
        away = turned(line, top)

        def strips(grad):
            packs = [pack(grad, side) for side in range(2)]
            out = [jnp.where(leave, value, 0.0) for leave, value in zip(leaves, packs)]
            stay = [jnp.where(leave, 0.0, value) for leave, value in zip(leaves, packs)]
            return jnp.where(left > HALO, out[0], out[1]), stay, [inner_of(part) for part in grad]

        grad = edge()
        gmsg_edge[s], stay, inner = strips(grad)
        start(gmsg_link[s], EDGE)
        for k in range(2):
            inner_out[s, k] = jnp.where(away, inner[k], 0.0)
            in_edge[s, k] = jnp.where(away, 0.0, inner[k])
        for link in ns[1][s][INNER]:
            link.start()
        for k in range(2):
            pack_out[s, k] = jnp.where(away, stay[k], 0.0)
            pack_edge[s, k] = jnp.where(away, 0.0, stay[k])
        gmsg_mid[s], stay, inner = strips(middle())
        if s == 0:
            start(gmsg_link[1], MID)
            start(gmsg_link[0], MID)
        for k in range(2):
            in_mid[s, k] = inner[k]
            pack_mid[s, k] = stay[k]

    def inside(value):
        return value[HALO : tile - HALO]

    def product(ar, ai, br, bi):
        return ar * br + ai * bi, ai * br - ar * bi

    if len(row_bits) > 1:
        add_rows(len(row_bits) - 1)
    rs_cols = col_copies(0)
    for copy in rs_cols:
        copy.start()

    fetches[5].wait()
    assemble(0)
    ar, ai = z[0, 0], z[0, 1]
    pr, pi = probe[0], probe[1]
    vr, vi = sandwich(pr * ar - pi * ai, pr * ai + pi * ar, table, 1, False)

    assemble(1)
    br, bi = z[1, 0], z[1, 1]
    wr, wi = sandwich(vr * br - vi * bi, vr * bi + vi * br, table, 0, False)
    fetches[8].wait()
    live = jnp.where(count[0] > 0, 2.0, 0.0)
    scale = live - (live * amp[...]) * lax.rsqrt(wr * wr + wi * wi + 1.0)
    xr, xi = sandwich(scale * wr, scale * wi, table, 0, True)
    back(1, *[(lambda cut=cut: product(*[cut(v) for v in (xr, xi, vr, vi)])) for cut in (ends, inside)])

    yr, yi = transform(*product(xr, xi, br, bi), table, 1, 0, True, True, True)
    for copy in rs_cols:
        copy.wait_recv()
    fetches[4].wait()
    total = prev[slot, col]
    for t in range(1, cols):
        total = total + buf2[t - 1]
    rate = PROBE_RATE / math.sqrt(rows * cols)
    out_probe[slot, col] = probe_piece[...] - rate * total
    ag_cols = col_copies(1)
    for copy in ag_cols:
        copy.start()


    u_parts = {}

    def object_grad(cut):
        u_parts[cut] = transform(cut(yr), cut(yi), table, 1, 1, True, True, True)
        return product(*u_parts[cut], cut(pr), cut(pi))

    back(0, lambda: object_grad(ends), lambda: object_grad(inside))
    ur, ui = [cat([e[:HALO], m, e[HALO:]], 0) for e, m in zip(u_parts[ends], u_parts[inside])]

    def relay(s, pieces):
        for p in pieces:
            gmsg_link[s][p].arrive()
            pass_link[s][p].start()

    relay(1, EDGE)
    for copy in ag_cols:
        copy.wait_recv()
    spread_rows(0)
    relay(0, EDGE)
    home_rows = lax.rem(tile + HALO - top, tile)
    home_cols = lax.rem(tile + HALO - left, tile)
    out_part[0] = pltpu.roll(pltpu.roll(ur * ar + ui * ai, home_rows, 0), home_cols, 1)
    out_part[1] = pltpu.roll(pltpu.roll(ui * ar - ur * ai, home_rows, 0), home_cols, 1)

    head_off, tail_off = off[0], off[1]
    accept = (head_off[1, :1] > HALO, tail_off[1, :1] < HALO)
    corner = (head_off[0, :1], tail_off[0, :1])

    def collect_edge(s):
        for h, rows_ in enumerate(halves_of):
            pass_link[s][EDGE[h]].arrive()
            kept = []
            for side in range(2):
                strip = jnp.where(accept[side], gs_edge[side, s, rows_], 0.0)
                moves = turned(line[rows_], corner[side])
                pack_out[s, side, rows_] += jnp.where(moves, strip, 0.0)
                kept.append(jnp.where(moves, 0.0, strip))
            ns[1][s][PACK][h].start()
            for side in range(2):
                pack_edge[s, side, rows_] += kept[side]

    def collect_mid(s):
        arrive(pass_link[s], MID)
        packs = [
            strip_mid[side, s] - OBJ_RATE * (pack_mid[s, side] + jnp.where(accept[side], gs_mid[side, s], 0.0))
            for side in range(2)
        ]
        inner = [inner_of(obj[s, k, HALO : tile - HALO, :]) - OBJ_RATE * in_mid[s, k] for k in range(2)]
        for k, value in enumerate(unpack(*packs, inner)):
            out_obj[s, k, HALO : tile - HALO, :] = value

    def finish_edge(s):
        for kind in (INNER, PACK):
            for link in ns[1][s][kind]:
                link.arrive()
        packs = [strip_edge[side, s] - OBJ_RATE * (pack_edge[s, side] + ns_pack[1, s, side]) for side in range(2)]
        inner = [inner_edge[s, k] - OBJ_RATE * (in_edge[s, k] + ns_inner[1, s, k]) for k in range(2)]
        for k, value in enumerate(unpack(*packs, inner)):
            out_obj[s, k, :HALO, :] = value[:HALO]
            out_obj[s, k, tile - HALO :, :] = value[HALO:]

    collect_edge(1)
    relay(1, MID)
    relay(0, MID)
    collect_edge(0)
    for held in range(1, rows // 2):
        spread_rows(held)
    collect_mid(1)
    collect_mid(0)
    finish_edge(1)
    for held in range(rows // 2, rows):
        spread_rows(held)
    finish_edge(0)

    off_near.sent()
    off_far.sent()
    for s in range(2):
        for phase in range(2):
            for link in ns[phase][s][PACK] + ns[phase][s][INNER]:
                link.sent()
        for piece in range(4):
            for group in (far_link, msg_link, gmsg_link, pass_link):
                group[s][piece].sent()
    for copy in row_down + rs_cols + ag_cols + list(row_up.values()):
        copy.wait_send()


def store(obj, probe, part, out_obj, out_probe, out_part, sem):
    copies = [
        pltpu.make_async_copy(src, dst, sem.at[k])
        for k, (src, dst) in enumerate(((obj, out_obj), (probe, out_probe), (part, out_part)))
    ]
    for copy in copies:
        copy.start()
    for copy in copies:
        copy.wait()


def shards(rows, cols, objects, probe, prev_partial, offsets, counts, amplitudes):
    tile = objects.shape[2]
    win = probe.shape[-1]
    assert tile == win == 4 * HALO and cols % 2 == 0
    piece = (2 * win) // (rows * cols)
    split_shape = (rows, cols, piece, win)
    table = jnp.asarray(operator_table(win))
    f32 = jnp.float32
    anyspace = pl.BlockSpec(memory_space=pl.ANY)
    vmem = pl.BlockSpec(memory_space=pltpu.VMEM)
    V = lambda *shape: pltpu.VMEM(shape, f32)
    mid, wide = tile - 2 * HALO, 2 * HALO
    dma = pltpu.SemaphoreType.DMA
    scratch = [
        V(2, 2, tile, tile), V(*split_shape), V(2, win, win), V(piece, win), V(win, win),
        pltpu.VMEM(table.shape, jnp.bfloat16),
        pltpu.VMEM((2, 8, wide), jnp.int32), pltpu.VMEM((2, 2, 8, wide), jnp.int32),
        V(2, 2, mid, wide), V(2, 2, wide, wide), V(2, 2, wide, wide), V(2, 2, 2, wide, wide), V(2, 2, 2, wide, wide),
        V(2, wide, wide),
        V(2, mid, wide), V(2, wide, wide), V(2, mid, wide), V(2, wide, wide), V(2, mid, wide), V(2, wide, wide),
        V(2, 2, tile, tile),
        V(2, mid, wide), V(2, wide, wide), V(2, 2, mid, wide), V(2, 2, wide, wide),
        V(2, 2, wide, wide), V(2, 2, wide, wide), V(2, 2, mid, wide), V(2, 2, wide, wide), V(2, 2, mid, wide), V(2, 2, wide, wide),
        V(max(rows - 1, 1), cols, piece, win), V(max(cols - 1, 1), piece, win),
        pltpu.SMEM((2,), jnp.int32), pltpu.SMEM((1,), jnp.int32), dma((9,)), dma((2,)), dma((2,)), dma((2, 2, 4)), dma((2, 2, 4)),
        dma((2, 2, 4)), dma((2, 2, 4)), dma((2, 2, 4)), dma((2, 2, 4)),
        dma((2, max(rows - 1, 1))), dma((2, max(rows - 1, 1))),
        dma((2, max(cols - 1, 1))), dma((2, max(cols - 1, 1))),
        pltpu.SemaphoreType.REGULAR((max(cols.bit_length() - 2, 1),)),
    ]
    results = pl.pallas_call(
        functools.partial(kernel, rows, cols),
        out_shape=(
            pltpu.VMEM(objects.shape, f32), pltpu.VMEM(split_shape, f32), pltpu.VMEM(probe.shape, f32),
        ),
        in_specs=[anyspace] * 8,
        out_specs=(vmem, vmem, vmem),
        scratch_shapes=scratch,
        compiler_params=pltpu.CompilerParams(
            collective_id=0, has_side_effects=True, vmem_limit_bytes=56 * 2**20
        ),
    )(
        offsets.reshape(2), counts.reshape(1), objects, prev_partial.reshape(split_shape),
        probe, probe.reshape(split_shape), amplitudes.reshape(win, win), table,
    )
    new_obj, new_probe, part = pl.pallas_call(
        store,
        out_shape=tuple(jax.ShapeDtypeStruct(v.shape, f32) for v in results),
        in_specs=[vmem] * 3,
        out_specs=(pl.BlockSpec(memory_space=pltpu.HBM),) * 3,
        scratch_shapes=[dma((3,))],
    )(*[pltpu.with_memory_space_constraint(v, pltpu.VMEM) for v in results])
    return new_obj, new_probe.reshape(probe.shape), part[None, None]


def solution(mesh):
    in_specs = (
        P(None, None, "row", "col"),
        P(),
        P("row", "col", None, None, None),
        P("row", "col", None, None),
        P("row", "col"),
        P("row", "col", None, None, None),
    )
    out_specs = (P(None, None, "row", "col"), P(), P("row", "col", None, None, None))
    body = functools.partial(shards, mesh.shape["row"], mesh.shape["col"])
    return jax.shard_map(body, mesh=mesh, in_specs=in_specs, out_specs=out_specs, check_vma=False)
```

```python
import functools
import math

import jax
import jax.numpy as jnp
import numpy as np
from jax import lax
from jax.experimental import pallas as pl
from jax.experimental.pallas import tpu as pltpu
from jax.sharding import PartitionSpec as P

HALO = 64
OBJ_RATE = 0.1
PROBE_RATE = 0.3
MESH = pl.DeviceIdType.MESH


def split(value):
    high = value.astype(jnp.bfloat16)
    low = (value - high.astype(jnp.float32)).astype(jnp.bfloat16)
    return high, low


def operator_table(n):
    half = n // 2
    index = np.arange(n)
    dft = np.exp(-2j * np.pi * (np.outer(index, index) % n) / n) / np.sqrt(n)
    freq = np.where(index < half, index, index - n).astype(np.float64)
    phase = np.exp(1j * np.pi * freq * freq / (4.0 * n))
    prop = np.conj(dft) @ (phase[:, None] * dft)
    near, far = prop[:half, :half], prop[:half, half:]
    tables = []
    for mat in (dft[0::2, :half], dft[1::2, :half], (near + far) / 2, (near - far) / 2):
        right = np.block([[mat.real.T, mat.imag.T], [-mat.imag.T, mat.real.T]]).astype(np.float32)
        for part in (right, right.T):
            high = part.astype(jnp.bfloat16)
            tables += [high, (part - high.astype(np.float32)).astype(jnp.bfloat16)]
    return np.stack(tables).reshape(2, 2, 2, 2, n, n)


def dot(left, right):
    return jnp.dot(left, right, preferred_element_type=jnp.float32)


def cat(parts, axis):
    return jnp.concatenate(parts, axis=axis)


def times(data, table, which, side, flip):
    kind = int(flip if side else not flip)
    out = []
    for k in range(2):
        high, low = table[which, k, kind, 0], table[which, k, kind, 1]
        dh, dl = split(data[k])
        if side:
            out.append(dot(cat([dh, dl, dh], 1), cat([high, high, low], 0)))
        else:
            out.append(dot(cat([high, high, low], 1), cat([dh, dl, dh], 0)))
    return out


def halves(value, axis):
    half = value.shape[axis] // 2
    return (value[:half], value[half:]) if axis == 0 else (value[:, :half], value[:, half:])


def transform(re, im, table, which, axis, merge, divide, flip):
    if divide:
        parts = [halves(v, axis) for v in (re, im)]
        data = [cat([a + b for a, b in parts], axis), cat([a - b for a, b in parts], axis)]
    else:
        parts = [halves(v, axis) for v in (re, im)]
        data = [cat([p[0] for p in parts], axis), cat([p[1] for p in parts], axis)]
    even, odd = [halves(v, axis) for v in times(data, table, which, axis, flip)]
    if merge:
        return [cat([a + b, a - b], axis) for a, b in zip(even, odd)]
    return [cat([a, b], axis) for a, b in zip(even, odd)]


def sandwich(xr, xi, table, which, conj):
    divide = which == 1 or not conj
    merge = which == 1 or conj
    tr, ti = transform(xr, xi, table, which, 1, merge, divide, conj)
    return transform(tr, ti, table, which, 0, merge, divide, conj)


def kernel(
    rows, cols, offs_hbm, count_hbm, obj_hbm, prev_hbm, probe_hbm, probe_k_hbm, amp_hbm, table_hbm,
    out_obj, out_probe, out_part,
    obj, prev, probe, probe_piece, amp, table,
    my_off, off,
    strip_mid, strip_edge, inner_edge, ns_pack, ns_inner, fold_far, far_mid, far_edge, msg_mid, msg_edge, got_mid, got_edge, z,
    gmsg_mid, gmsg_edge, gs_mid, gs_edge, pack_out, inner_out, pack_mid, pack_edge, in_mid, in_edge,
    buf1, buf2,
    offs, count, local_sem, off_send, off_recv, ns_send, ns_recv, far_send, far_recv, msg_send, msg_recv,
    row_send, row_recv, col_send, col_recv, known,
):
    tile = obj.shape[2]
    mid_rows = tile - 2 * HALO
    wide = 2 * HALO
    row, col = lax.axis_index("row"), lax.axis_index("col")
    odd = lax.rem(col, 2)
    step = 1 - 2 * odd
    near = 1 - odd
    far = odd
    partner, other = col + step, col - step
    ahead, behind = col + 2 * step, col - 2 * step
    has_other = (other >= 0) & (other < cols)
    has_ahead = (ahead >= 0) & (ahead < cols)
    has_behind = (behind >= 0) & (behind < cols)
    has_north, has_south = row > 0, row < rows - 1
    always = row >= 0

    def flip(value, bit):
        return value + bit * (1 - 2 * lax.rem(value // bit, 2))

    row_bits = [1 << k for k in range(rows.bit_length() - 1)]
    base, length, row_down, row_keep = 0, rows, [], []
    for k, bit in enumerate(row_bits):
        length = length // 2
        upper = lax.rem(row // bit, 2)
        keep, give = base + upper * length, base + (1 - upper) * length
        landing = buf1.at[pl.ds(rows - 2 * length, length)]
        row_down.append(pltpu.make_async_remote_copy(
            src_ref=prev.at[pl.ds(give, length)], dst_ref=landing, send_sem=row_send.at[0, k],
            recv_sem=row_recv.at[0, k], device_id=(flip(row, bit), col), device_id_type=MESH))
        row_keep.append((keep, length, landing))
        base = keep
    slot = base
    row_up = {}
    for k, bit in enumerate(reversed(row_bits)):
        for held in range(1 << k):
            where = slot
            for t in range(k):
                where = flip(where, 1 << t) if held >> t & 1 else where
            here, index = out_probe.at[where], held | 1 << k
            row_up[index] = pltpu.make_async_remote_copy(
                src_ref=here, dst_ref=here, send_sem=row_send.at[1, index - 1],
                recv_sem=row_recv.at[1, index - 1], device_id=(flip(row, bit), col), device_id_type=MESH)

    def spread_rows(held):
        if held:
            row_up[held].wait_recv()
        for k in range(held.bit_length(), len(row_bits)):
            row_up[held | 1 << k].start()

    fetches = [
        pltpu.make_async_copy(src, dst, local_sem.at[k])
        for k, (src, dst) in enumerate(
            ((obj_hbm.at[0], obj.at[0]), (obj_hbm.at[1], obj.at[1]), (prev_hbm, prev),
             (probe_hbm, probe), (probe_k_hbm.at[slot, col], probe_piece),
             (table_hbm, table), (amp_hbm, amp), (offs_hbm, offs), (count_hbm, count))
        )
    ]
    for k in (7, 0, 1, 2):
        fetches[k].start()

    barrier = pltpu.get_barrier_semaphore()

    def greet(sem, r, c):
        pl.semaphore_signal(sem, inc=1, device_id=(r, c), device_id_type=MESH)

    bits = [1 << k for k in range(cols.bit_length() - 1)]
    expected = 0
    for t in range(1, rows):
        greet(barrier, lax.rem(row + t, rows), col)
        expected = expected + 1
    for ok, c in ((always, partner), (has_other, other), (has_ahead, ahead), (has_behind, behind)):
        @pl.when(ok)
        def _():
            greet(barrier, row, c)
        expected = expected + ok.astype(jnp.int32)
    for bit in bits[2:]:
        greet(barrier, row, flip(col, bit))
        expected = expected + 1

    fetches[7].wait()
    top, left = offs[0], offs[1]
    my_off[0] = jnp.zeros((8, wide), jnp.int32) + top
    my_off[1] = jnp.zeros((8, wide), jnp.int32) + left

    lane = lax.broadcasted_iota(jnp.int32, (1, wide), 1)
    first = lane < HALO
    lane64 = jnp.where(first, lane, lane - HALO)
    line = lax.broadcasted_iota(jnp.int32, (wide, 1), 0)

    def swap(value):
        return pltpu.roll(value, HALO, 1)

    def turned(index, corner):
        return (index < corner - HALO) | (index >= corner + HALO)

    def pack(ref, slot):
        re, im = ref
        if slot == 0:
            return jnp.where(first, re[:, :wide], swap(im[:, :wide]))
        return jnp.where(first, swap(re[:, tile - wide :]), im[:, tile - wide :])

    def inner_of(value):
        return jnp.where(first, value[:, wide:], value[:, :wide])

    def unpack(head, tail, inner):
        re = cat([jnp.where(first, head, inner[0]), jnp.where(first, inner[0], swap(tail))], 1)
        im = cat([jnp.where(first, swap(head), inner[1]), jnp.where(first, inner[1], tail)], 1)
        return re, im

    def ends(value):
        return cat([value[:HALO], value[tile - HALO :]], 0)

    class Link:
        def __init__(self, src, dst, send_sem, recv_sem, device, ok, inbound):
            self.copy = pltpu.make_async_remote_copy(
                src_ref=src, dst_ref=dst, send_sem=send_sem, recv_sem=recv_sem,
                device_id=device, device_id_type=MESH)
            self.ok, self.inbound = ok, inbound

        def start(self):
            @pl.when(self.ok)
            def _():
                self.copy.start()

        def arrive(self):
            @pl.when(self.inbound)
            def _():
                self.copy.wait_recv()

        def sent(self):
            @pl.when(self.ok)
            def _():
                self.copy.wait_send()

    up, down = slice(0, HALO), slice(HALO, wide)
    off_near = Link(my_off, off.at[1 - near], off_send.at[0], off_recv.at[0], (row, partner), always, always)
    off_far = Link(my_off, off.at[1 - far], off_send.at[1], off_recv.at[1], (row, other), has_other, has_other)

    north, south = (row - 1, has_north, has_south), (row + 1, has_south, has_north)

    def ns_links(phase, s, kind):
        if kind == 0:
            src = strip_edge.at[:, s] if phase == 0 else pack_out.at[s]
            dst = ns_pack.at[phase, s]
        else:
            src = (inner_edge if phase == 0 else inner_out).at[s]
            dst = ns_inner.at[phase, s]
        made = []
        for k, (span, to) in enumerate(((up, south if phase else north), (down, north if phase else south))):
            sem = 2 * kind + k
            made.append(Link(src.at[:, span, :], dst.at[:, span, :], ns_send.at[phase, s, sem], ns_recv.at[phase, s, sem],
                             (to[0], col), to[1], to[2]))
        return made

    PACK, INNER = 0, 1
    ns = [[[ns_links(phase, s, kind) for kind in range(2)] for s in range(2)] for phase in range(2)]
    MID, EDGE = (0, 1), (2, 3)
    halves_of = (slice(0, HALO), slice(HALO, wide))

    def chunks(make):
        return [[make(s, p, p // 2, halves_of[p % 2]) for p in range(4)] for s in range(2)]

    far_link = chunks(lambda s, p, b, rows_: Link(
        fold_far.at[s, rows_] if b else strip_mid.at[far, s, rows_], (far_mid, far_edge)[b].at[s, rows_],
        far_send.at[0, s, p], far_recv.at[0, s, p], (row, behind), has_behind, has_ahead))
    msg_link = chunks(lambda s, p, b, rows_: Link(
        (msg_mid, msg_edge)[b].at[s, rows_], (got_mid, got_edge)[b].at[s, rows_],
        msg_send.at[0, s, p], msg_recv.at[0, s, p], (row, partner), always, always))
    gmsg_link = chunks(lambda s, p, b, rows_: Link(
        (gmsg_mid, gmsg_edge)[b].at[s, rows_], (gs_mid, gs_edge)[b].at[1 - near, s, rows_],
        msg_send.at[1, s, p], msg_recv.at[1, s, p], (row, partner), always, always))
    pass_link = chunks(lambda s, p, b, rows_: Link(
        (gs_mid, gs_edge)[b].at[near, s, rows_], (gs_mid, gs_edge)[b].at[far, s, rows_],
        far_send.at[1, s, p], far_recv.at[1, s, p], (row, ahead), has_ahead, has_behind))

    def start(links, pieces):
        for p in pieces:
            links[p].start()

    def arrive(links, pieces):
        for p in pieces:
            links[p].arrive()

    def add_rows(k):
        keep, count_rows, landing = row_keep[k]
        row_down[k].wait_recv()
        prev[pl.ds(keep, count_rows)] += landing[...]

    def col_copies(stage):
        made = []
        for t in range(1, cols):
            peer = lax.rem(col + t, cols)
            if stage == 0:
                src, dst = prev.at[slot, peer], buf2.at[t - 1]
            else:
                src, dst = out_probe.at[slot, col], out_probe.at[slot, col]
            made.append(pltpu.make_async_remote_copy(
                src_ref=src, dst_ref=dst, send_sem=col_send.at[stage, t - 1],
                recv_sem=col_recv.at[stage, t - 1], device_id=(row, peer), device_id_type=MESH))
        return made

    def pack_slice(s):
        fetches[s].wait()
        for side in range(2):
            value = pack((obj[s, 0], obj[s, 1]), side)
            strip_mid[side, s] = value[HALO : tile - HALO]
            strip_edge[side, s] = ends(value)

    pack_slice(0)
    pl.semaphore_wait(barrier, expected)
    off_near.start()
    off_far.start()
    for link in ns[0][0][PACK]:
        link.start()
    start(far_link[0], MID)
    fetches[2].wait()
    row_down[0].start()
    pack_slice(1)
    for link in ns[0][1][PACK]:
        link.start()
    start(far_link[1], MID)
    for bit in bits:
        greet(known.at[0], row, flip(col, bit))
    for k in (3, 4, 5, 6, 8):
        fetches[k].start()

    @pl.when(jnp.logical_not(has_other))
    def _():
        off[far] = jnp.full((2, 8, wide), HALO, jnp.int32)

    for s in range(2):
        for phase, spans in ((0, ((has_south, slice(0, HALO)), (has_north, slice(HALO, wide)))),
                             (1, ((has_north, slice(0, HALO)), (has_south, slice(HALO, wide))))):
            for ok, span in spans:
                @pl.when(jnp.logical_not(ok))
                def _():
                    ns_pack[phase, s, :, span, :] = jnp.zeros((2, HALO, wide), jnp.float32)
                    ns_inner[phase, s, :, span, :] = jnp.zeros((2, HALO, wide), jnp.float32)

        @pl.when(jnp.logical_not(has_ahead))
        def _():
            far_mid[s] = jnp.zeros((mid_rows, wide), jnp.float32)
            far_edge[s] = jnp.zeros((wide, wide), jnp.float32)

        @pl.when(jnp.logical_not(has_behind))
        def _():
            gs_mid[far, s] = jnp.zeros((mid_rows, wide), jnp.float32)
            gs_edge[far, s] = jnp.zeros((wide, wide), jnp.float32)

    off_near.arrive()
    off_far.arrive()
    near_off, far_off = off[near], off[far]
    near_top, near_left = near_off[0, :1], near_off[1, :1]
    far_top = far_off[0, :1]
    take_own = jnp.where(near == 0, near_left - HALO, HALO - near_left) > 0

    def fold(s):
        for h, rows_ in enumerate(halves_of):
            ns[0][s][PACK][h].arrive()
            fold_far[s, rows_] = jnp.where(turned(line[rows_], far_top), ns_pack[0, s, far, rows_], strip_edge[far, s, rows_])
            far_link[s][EDGE[h]].start()
        for rows_ in halves_of:
            msg_edge[s, rows_] = jnp.where(turned(line[rows_], near_top), ns_pack[0, s, near, rows_], strip_edge[near, s, rows_])

    def forward_mid(s):
        for p, rows_ in zip(MID, halves_of):
            far_link[s][p].arrive()
            msg_mid[s, rows_] = jnp.where(take_own, strip_mid[near, s, rows_], far_mid[s, rows_])
            msg_link[s][p].start()

    def forward_edge(s):
        for p, rows_ in zip(EDGE, halves_of):
            far_link[s][p].arrive()
            msg_edge[s, rows_] = jnp.where(take_own, msg_edge[s, rows_], far_edge[s, rows_])
            msg_link[s][p].start()

    add_rows(0)
    for k in range(1, len(row_bits)):
        row_down[k].start()
        if k + 1 < len(row_bits):
            add_rows(k)
    for s in range(2):
        for k in range(2):
            inner_edge[s, k] = inner_of(ends(obj[s, k]))
        for link in ns[0][s][INNER]:
            link.start()
    fold(0)
    forward_mid(0)
    fold(1)
    forward_mid(1)
    fetches[3].wait()
    turn_rows = lax.rem(top + tile - HALO, tile)
    turn_cols = lax.rem(left + tile - HALO, tile)
    for k in range(2):
        probe[k] = pltpu.roll(pltpu.roll(probe[k], turn_rows, 0), turn_cols, 1)

    fetches[6].wait()
    count_half = tile // 2

    def order(axis):
        target = lax.broadcasted_iota(jnp.int32, (tile, tile), axis)
        source = lax.broadcasted_iota(jnp.int32, (tile, tile), 1 - axis)
        target = jnp.where(target < count_half, 2 * target, 2 * (target - count_half) + 1)
        return (source == target).astype(jnp.float32).astype(jnp.bfloat16)

    ordered = dot(cat([order(0), order(0)], 1), cat(split(amp[...]), 0))
    amp[...] = dot(cat(split(ordered), 1), cat([order(1), order(1)], 0))

    forward_edge(0)
    forward_edge(1)

    for wait_round, bit in enumerate(bits[1:]):
        pl.semaphore_wait(known.at[wait_round], len(bits))
        if wait_round + 1 < len(bits) - 1:
            for again in bits:
                greet(known.at[wait_round + 1], row, flip(col, again))

    def assemble(s):
        from_east, from_west = lane64 < left - HALO, lane64 >= left

        arrive(msg_link[s], MID)
        packs = [jnp.where(take, got_mid[s], strip_mid[side, s]) for side, take in enumerate((from_east, from_west))]
        inner = [inner_of(obj[s, k, HALO : tile - HALO, :]) for k in range(2)]
        for k, value in enumerate(unpack(*packs, inner)):
            z[s, k, HALO : tile - HALO, :] = value
        for link in ns[0][s][INNER]:
            link.arrive()
        away = turned(line, top)
        inner = [jnp.where(away, ns_inner[0, s, k], inner_edge[s, k]) for k in range(2)]
        packs = [jnp.where(away, ns_pack[0, s, side], strip_edge[side, s]) for side in range(2)]
        arrive(msg_link[s], EDGE)
        packs = [jnp.where(take, got_edge[s], packs[side]) for side, take in enumerate((from_east, from_west))]
        for k, value in enumerate(unpack(*packs, inner)):
            z[s, k, :HALO, :] = value[:HALO]
            z[s, k, tile - HALO :, :] = value[HALO:]

    def back(s, edge, middle):
        leaves = lane64 < left - HALO, lane64 >= left
        away = turned(line, top)

        def strips(grad):
            packs = [pack(grad, side) for side in range(2)]
            out = [jnp.where(leave, value, 0.0) for leave, value in zip(leaves, packs)]
            stay = [jnp.where(leave, 0.0, value) for leave, value in zip(leaves, packs)]
            return jnp.where(left > HALO, out[0], out[1]), stay, [inner_of(part) for part in grad]

        grad = edge()
        gmsg_edge[s], stay, inner = strips(grad)
        start(gmsg_link[s], EDGE)
        for k in range(2):
            inner_out[s, k] = jnp.where(away, inner[k], 0.0)
            in_edge[s, k] = jnp.where(away, 0.0, inner[k])
        for link in ns[1][s][INNER]:
            link.start()
        for k in range(2):
            pack_out[s, k] = jnp.where(away, stay[k], 0.0)
            pack_edge[s, k] = jnp.where(away, 0.0, stay[k])
        gmsg_mid[s], stay, inner = strips(middle())
        if s == 0:
            start(gmsg_link[1], MID)
            start(gmsg_link[0], MID)
        for k in range(2):
            in_mid[s, k] = inner[k]
            pack_mid[s, k] = stay[k]

    def inside(value):
        return value[HALO : tile - HALO]

    def product(ar, ai, br, bi):
        return ar * br + ai * bi, ai * br - ar * bi

    if len(row_bits) > 1:
        add_rows(len(row_bits) - 1)
    rs_cols = col_copies(0)
    for copy in rs_cols:
        copy.start()

    fetches[5].wait()
    assemble(0)
    ar, ai = z[0, 0], z[0, 1]
    pr, pi = probe[0], probe[1]
    vr, vi = sandwich(pr * ar - pi * ai, pr * ai + pi * ar, table, 1, False)

    assemble(1)
    br, bi = z[1, 0], z[1, 1]
    wr, wi = sandwich(vr * br - vi * bi, vr * bi + vi * br, table, 0, False)
    fetches[8].wait()
    live = jnp.where(count[0] > 0, 2.0, 0.0)
    scale = live - (live * amp[...]) * lax.rsqrt(wr * wr + wi * wi + 1.0)
    xr, xi = sandwich(scale * wr, scale * wi, table, 0, True)
    back(1, *[(lambda cut=cut: product(*[cut(v) for v in (xr, xi, vr, vi)])) for cut in (ends, inside)])

    yr, yi = transform(*product(xr, xi, br, bi), table, 1, 0, True, True, True)
    for copy in rs_cols:
        copy.wait_recv()
    fetches[4].wait()
    total = prev[slot, col]
    for t in range(1, cols):
        total = total + buf2[t - 1]
    rate = PROBE_RATE / math.sqrt(rows * cols)
    out_probe[slot, col] = probe_piece[...] - rate * total
    ag_cols = col_copies(1)
    for copy in ag_cols:
        copy.start()


    u_parts = {}

    def object_grad(cut):
        u_parts[cut] = transform(cut(yr), cut(yi), table, 1, 1, True, True, True)
        return product(*u_parts[cut], cut(pr), cut(pi))

    back(0, lambda: object_grad(ends), lambda: object_grad(inside))
    ur, ui = [cat([e[:HALO], m, e[HALO:]], 0) for e, m in zip(u_parts[ends], u_parts[inside])]

    def relay(s, pieces):
        for p in pieces:
            gmsg_link[s][p].arrive()
            pass_link[s][p].start()

    relay(1, EDGE)
    for copy in ag_cols:
        copy.wait_recv()
    spread_rows(0)
    relay(0, EDGE)
    head_off, tail_off = off[0], off[1]
    accept = (head_off[1, :1] > HALO, tail_off[1, :1] < HALO)
    corner = (head_off[0, :1], tail_off[0, :1])

    def collect_edge(s):
        for h, rows_ in enumerate(halves_of):
            pass_link[s][EDGE[h]].arrive()
            kept = []
            for side in range(2):
                strip = jnp.where(accept[side], gs_edge[side, s, rows_], 0.0)
                moves = turned(line[rows_], corner[side])
                pack_out[s, side, rows_] += jnp.where(moves, strip, 0.0)
                kept.append(jnp.where(moves, 0.0, strip))
            ns[1][s][PACK][h].start()
            for side in range(2):
                pack_edge[s, side, rows_] += kept[side]

    def collect_mid(s):
        arrive(pass_link[s], MID)
        packs = [
            strip_mid[side, s] - OBJ_RATE * (pack_mid[s, side] + jnp.where(accept[side], gs_mid[side, s], 0.0))
            for side in range(2)
        ]
        inner = [inner_of(obj[s, k, HALO : tile - HALO, :]) - OBJ_RATE * in_mid[s, k] for k in range(2)]
        for k, value in enumerate(unpack(*packs, inner)):
            out_obj[s, k, HALO : tile - HALO, :] = value

    def finish_edge(s):
        for kind in (INNER, PACK):
            for link in ns[1][s][kind]:
                link.arrive()
        packs = [strip_edge[side, s] - OBJ_RATE * (pack_edge[s, side] + ns_pack[1, s, side]) for side in range(2)]
        inner = [inner_edge[s, k] - OBJ_RATE * (in_edge[s, k] + ns_inner[1, s, k]) for k in range(2)]
        for k, value in enumerate(unpack(*packs, inner)):
            out_obj[s, k, :HALO, :] = value[:HALO]
            out_obj[s, k, tile - HALO :, :] = value[HALO:]

    collect_edge(1)
    relay(1, MID)
    relay(0, MID)
    collect_edge(0)
    for held in range(1, rows // 2):
        spread_rows(held)
    home_rows = lax.rem(tile + HALO - top, tile)
    home_cols = lax.rem(tile + HALO - left, tile)
    out_part[0] = pltpu.roll(pltpu.roll(ur * ar + ui * ai, home_rows, 0), home_cols, 1)
    out_part[1] = pltpu.roll(pltpu.roll(ui * ar - ur * ai, home_rows, 0), home_cols, 1)

    collect_mid(1)
    collect_mid(0)
    finish_edge(1)
    for held in range(rows // 2, rows):
        spread_rows(held)
    finish_edge(0)

    off_near.sent()
    off_far.sent()
    for s in range(2):
        for phase in range(2):
            for link in ns[phase][s][PACK] + ns[phase][s][INNER]:
                link.sent()
        for piece in range(4):
            for group in (far_link, msg_link, gmsg_link, pass_link):
                group[s][piece].sent()
    for copy in row_down + rs_cols + ag_cols + list(row_up.values()):
        copy.wait_send()


def store(obj, probe, part, out_obj, out_probe, out_part, sem):
    copies = [
        pltpu.make_async_copy(src, dst, sem.at[k])
        for k, (src, dst) in enumerate(((obj, out_obj), (probe, out_probe), (part, out_part)))
    ]
    for copy in copies:
        copy.start()
    for copy in copies:
        copy.wait()


def shards(rows, cols, objects, probe, prev_partial, offsets, counts, amplitudes):
    tile = objects.shape[2]
    win = probe.shape[-1]
    assert tile == win == 4 * HALO and cols % 2 == 0
    piece = (2 * win) // (rows * cols)
    split_shape = (rows, cols, piece, win)
    table = jnp.asarray(operator_table(win))
    f32 = jnp.float32
    anyspace = pl.BlockSpec(memory_space=pl.ANY)
    vmem = pl.BlockSpec(memory_space=pltpu.VMEM)
    V = lambda *shape: pltpu.VMEM(shape, f32)
    mid, wide = tile - 2 * HALO, 2 * HALO
    dma = pltpu.SemaphoreType.DMA
    scratch = [
        V(2, 2, tile, tile), V(*split_shape), V(2, win, win), V(piece, win), V(win, win),
        pltpu.VMEM(table.shape, jnp.bfloat16),
        pltpu.VMEM((2, 8, wide), jnp.int32), pltpu.VMEM((2, 2, 8, wide), jnp.int32),
        V(2, 2, mid, wide), V(2, 2, wide, wide), V(2, 2, wide, wide), V(2, 2, 2, wide, wide), V(2, 2, 2, wide, wide),
        V(2, wide, wide),
        V(2, mid, wide), V(2, wide, wide), V(2, mid, wide), V(2, wide, wide), V(2, mid, wide), V(2, wide, wide),
        V(2, 2, tile, tile),
        V(2, mid, wide), V(2, wide, wide), V(2, 2, mid, wide), V(2, 2, wide, wide),
        V(2, 2, wide, wide), V(2, 2, wide, wide), V(2, 2, mid, wide), V(2, 2, wide, wide), V(2, 2, mid, wide), V(2, 2, wide, wide),
        V(max(rows - 1, 1), cols, piece, win), V(max(cols - 1, 1), piece, win),
        pltpu.SMEM((2,), jnp.int32), pltpu.SMEM((1,), jnp.int32), dma((9,)), dma((2,)), dma((2,)), dma((2, 2, 4)), dma((2, 2, 4)),
        dma((2, 2, 4)), dma((2, 2, 4)), dma((2, 2, 4)), dma((2, 2, 4)),
        dma((2, max(rows - 1, 1))), dma((2, max(rows - 1, 1))),
        dma((2, max(cols - 1, 1))), dma((2, max(cols - 1, 1))),
        pltpu.SemaphoreType.REGULAR((max(cols.bit_length() - 2, 1),)),
    ]
    results = pl.pallas_call(
        functools.partial(kernel, rows, cols),
        out_shape=(
            pltpu.VMEM(objects.shape, f32), pltpu.VMEM(split_shape, f32), pltpu.VMEM(probe.shape, f32),
        ),
        in_specs=[anyspace] * 8,
        out_specs=(vmem, vmem, vmem),
        scratch_shapes=scratch,
        compiler_params=pltpu.CompilerParams(
            collective_id=0, has_side_effects=True, vmem_limit_bytes=56 * 2**20
        ),
    )(
        offsets.reshape(2), counts.reshape(1), objects, prev_partial.reshape(split_shape),
        probe, probe.reshape(split_shape), amplitudes.reshape(win, win), table,
    )
    new_obj, new_probe, part = pl.pallas_call(
        store,
        out_shape=tuple(jax.ShapeDtypeStruct(v.shape, f32) for v in results),
        in_specs=[vmem] * 3,
        out_specs=(pl.BlockSpec(memory_space=pltpu.HBM),) * 3,
        scratch_shapes=[dma((3,))],
    )(*[pltpu.with_memory_space_constraint(v, pltpu.VMEM) for v in results])
    return new_obj, new_probe.reshape(probe.shape), part[None, None]


def solution(mesh):
    in_specs = (
        P(None, None, "row", "col"),
        P(),
        P("row", "col", None, None, None),
        P("row", "col", None, None),
        P("row", "col"),
        P("row", "col", None, None, None),
    )
    out_specs = (P(None, None, "row", "col"), P(), P("row", "col", None, None, None))
    body = functools.partial(shards, mesh.shape["row"], mesh.shape["col"])
    return jax.shard_map(body, mesh=mesh, in_specs=in_specs, out_specs=out_specs, check_vma=False)
```
